128 devices in a mesh: dp: 32 (over y, x, core), tensor: 4 (over z).
Axes of the slice: x: 4, y: 4, z: 4, core: 2. Of those that a mesh axis runs over, the one named last changes fastest.
Arguments:
- tokens: bfloat16 [20480, 1152], P(('dp', 'tensor')), may hold values from -6 to 6
- cotangent: bfloat16 [20480, 1152], P(('dp', 'tensor')), may hold values from -24 to 24
- segment_ids: int32 [32, 640], P('dp'), may hold values from 0 to 3, as said below
- positions: int32 [32, 640], P('dp'), may hold values from 0 to 1999, as said below
- w_query: bfloat16 [1152, 1024], P('dp', 'tensor')
- w_key: bfloat16 [1152, 256], P('dp')
- w_value: bfloat16 [1152, 256], P('dp'), may hold values from -0.1875 to 0.1875
- w_out: bfloat16 [1024, 1152], P('tensor', 'dp'), may hold values from -0.1875 to 0.1875
- w_gate: bfloat16 [1152, 6912], P('dp', 'tensor'), may hold values from -0.1875 to 0.1875
- w_up: bfloat16 [1152, 6912], P('dp', 'tensor'), may hold values from -0.1875 to 0.1875
- w_down: bfloat16 [6912, 1152], P('tensor', 'dp'), may hold values from -0.078125 to 0.078125
- prenorm_attn: bfloat16 [1152], P('dp'), may hold values from 0.099609375 to 1.8984375
- postnorm_attn: bfloat16 [1152], P('dp'), may hold values from 0.099609375 to 1.8984375
- prenorm_ffw: bfloat16 [1152], P('dp'), may hold values from 0.099609375 to 1.8984375
- postnorm_ffw: bfloat16 [1152], P('dp'), may hold values from 0.099609375 to 1.8984375
- query_norm: bfloat16 [256], P('dp'), may hold values from 0.6 to 5
- key_norm: bfloat16 [256], P('dp'), may hold values from 0.6 to 5
Outputs:
- layer_out: bfloat16 [20480, 1152], P(('dp', 'tensor'))
- grad_tokens: float32 [20480, 1152], P(('dp', 'tensor'))
- grad_query: float32 [1152, 1024], P('dp', 'tensor')
- grad_key: float32 [1152, 256], P('dp')
- grad_value: float32 [1152, 256], P('dp')
- grad_output: float32 [1024, 1152], P('tensor', 'dp')
- grad_gate: float32 [1152, 6912], P('dp', 'tensor')
- grad_up: float32 [1152, 6912], P('dp', 'tensor')
- grad_down: float32 [6912, 1152], P('tensor', 'dp')
- grad_prenorm_attn: float32 [1152], P('dp')
- grad_postnorm_attn: float32 [1152], P('dp')
- grad_prenorm_ffw: float32 [1152], P('dp')
- grad_postnorm_ffw: float32 [1152], P('dp')
- grad_query_norm: float32 [256], P('dp')
- grad_key_norm: float32 [256], P('dp')
The draws below stay inside these ranges and needn't reach their ends.
Inputs may be any that keep to these rules, and one draw needn't show every extreme that they name: `segment_ids`: within each sequence the numbers never fall; a document is a run of equal numbers. Within a document positions rise by one from token to token.
All inputs are finite; a program needn't handle non-finite values.
Results may differ from the reference program's by a relative error of at most 0.033.
The reference program's roundings to bfloat16 on the way count: a program that leaves them out, or rounds other values in their place, can miss the bound.
Values may be sent and summed in bfloat16 or wider, within the bound.
A program may use at most 128 MiB of HBM per device.

```python
import math
import jax
import jax.numpy as jnp
from jax import lax

D = 1152
HEADS = 4
HD = 256
FF = 6912
WINDOW = 512
LEN = 640
SEQS = 32
TOKENS = 20480


def layout_rows(key):
    row_keys = jax.random.split(jax.random.fold_in(key, 17), SEQS)

    def single(row_key):
        key_len, key_start, key_cut = jax.random.split(row_key, 3)
        long_len = jax.random.randint(key_len, (), WINDOW + 32, LEN - 7)
        start = jax.random.randint(key_start, (), 1, LEN - long_len)
        stop = start + long_len
        cut = stop + jax.random.randint(key_cut, (), 0, LEN - stop)
        offset = 2000 - start
        index = jnp.arange(LEN, dtype=jnp.int32)
        segments = (index >= start).astype(jnp.int32) + (index >= stop).astype(jnp.int32) + (index >= cut).astype(jnp.int32)
        begin = jnp.where(index >= cut, cut, jnp.where(index >= stop, stop, jnp.where(index >= start, start, 0)))
        places = index - begin + jnp.where(index < start, offset, 0)
        return (segments.astype(jnp.int32), places.astype(jnp.int32))
    return jax.vmap(single)(row_keys)


def draw_segment_ids(key, part):
    return layout_rows(key)[0]


def draw_positions(key, part):
    return layout_rows(key)[1]


def key_matrix(key):
    return jax.random.normal(jax.random.fold_in(key, 29), (D, HD), jnp.float32) / math.sqrt(D)


def draw_w_key(key, part):
    return key_matrix(key).astype(jnp.bfloat16)


def draw_w_query(key, part):
    base = jax.random.normal(jax.random.fold_in(key, 31), (D, HEADS * HD), jnp.float32) / math.sqrt(D)
    return base.astype(jnp.bfloat16)


def draw_query_norm(key, part):
    values = jax.random.uniform(jax.random.fold_in(key, 37), (HD,), jnp.float32, 0.6, 1.6)
    return values.astype(jnp.bfloat16)


def draw_key_norm(key, part):
    values = jax.random.uniform(jax.random.fold_in(key, 41), (HD,), jnp.float32, 0.6, 1.6)
    return values.astype(jnp.bfloat16)


def raised(array, key, source, target, parts, factor):
    owner, partner = [(jnp.arange(array.shape[axis_at]) // (array.shape[axis_at] // parts)).reshape([-1 if axis == axis_at else 1 for axis in range(array.ndim)]) for axis_at in (source, target)]
    chosen = jax.random.permutation(key, parts)[partner]
    strong = (owner == chosen) | (owner == (partner + parts // 2) % parts)
    return jnp.where(strong, factor * array, array)


def levels(own_key, dims, cuts, least, top_value):
    def one(dim, parts):
        steps = jax.random.uniform(jax.random.fold_in(jax.random.fold_in(own_key, 6), dim), (parts,), jnp.float32, least / len(cuts), top_value / len(cuts))
        return jnp.repeat(jnp.exp(steps), dims[dim] // parts).reshape((-1,) + (1,) * (len(dims) - dim - 1))

    level = one(*cuts[0])
    for cut in cuts[1:]:
        level = level * one(*cut)
    return level


def centred(rng, dims, scale, limit, pieces=(), held_as=jnp.bfloat16):
    values = scale * jax.random.normal(rng, dims, jnp.float32)
    if pieces:
        values = values * levels(rng, dims, pieces, -0.22, 0.18)
    return jnp.clip(values, -limit, limit).astype(held_as)


def gaussian_with(rng, dims, spread, limit, shards, heavy, kind=jnp.bfloat16):
    drawn = spread * jax.random.normal(rng, dims, jnp.float32)
    if shards:
        drawn = drawn * levels(rng, dims, shards, -0.22, 0.18)
    return jnp.clip(raised(drawn, jax.random.fold_in(rng, 3), *heavy), -limit, limit).astype(kind)


def setup_inputs(seed: int = 0) -> dict:
    key_list = jax.random.split(jax.random.key(seed), 18)
    return {
        "tokens": centred(key_list[0], (TOKENS, D), 1.0, 6.0, ((0, 128),)),
        "cotangent": gaussian_with(key_list[1], (TOKENS, D), 1.0, 24.0, ((0, 128),), (0, 1, 128, 5.5)),
        "segment_ids": draw_segment_ids(jax.random.fold_in(key_list[17], 71), 0),
        "positions": draw_positions(jax.random.fold_in(key_list[17], 71), 0),
        "w_query": draw_w_query(jax.random.fold_in(key_list[17], 71), 0),
        "w_key": draw_w_key(jax.random.fold_in(key_list[17], 71), 0),
        "w_value": centred(key_list[6], (D, HD), D ** -0.5, 0.1875, ((0, 32),)),
        "w_out": centred(key_list[7], (HEADS * HD, D), (HEADS * HD) ** -0.5, 0.1875, ((0, 4), (1, 32))),
        "w_gate": centred(key_list[8], (D, FF), D ** -0.5, 0.1875, ((0, 32), (1, 4))),
        "w_up": centred(key_list[9], (D, FF), D ** -0.5, 0.1875, ((0, 32), (1, 4))),
        "w_down": centred(key_list[10], (FF, D), FF ** -0.5, 0.078125, ((0, 4), (1, 32))),
        "prenorm_attn": jnp.clip(1.0 + 0.18 * jax.random.normal(key_list[11], (D,), jnp.float32), 0.099609375, 1.8984375).astype(jnp.bfloat16),
        "postnorm_attn": jnp.clip(1.0 + 0.18 * jax.random.normal(key_list[12], (D,), jnp.float32), 0.099609375, 1.8984375).astype(jnp.bfloat16),
        "prenorm_ffw": jnp.clip(1.0 + 0.18 * jax.random.normal(key_list[13], (D,), jnp.float32), 0.099609375, 1.8984375).astype(jnp.bfloat16),
        "postnorm_ffw": jnp.clip(1.0 + 0.18 * jax.random.normal(key_list[14], (D,), jnp.float32), 0.099609375, 1.8984375).astype(jnp.bfloat16),
        "query_norm": draw_query_norm(jax.random.fold_in(key_list[17], 71), 0),
        "key_norm": draw_key_norm(jax.random.fold_in(key_list[17], 71), 0),
    }


EPSILON = 1e-06
ROPE_BASE = 10000.0
GELU_SCALE = math.sqrt(2.0 / math.pi)
MASKED = -1e+30

def normalize(inputs):
    inverse = lax.rsqrt(lax.optimization_barrier(jnp.mean(inputs * inputs, axis=-1, keepdims=True)) + EPSILON)
    return (inputs * inverse, inverse)

def normalize_back(grad_hat, normed, inverse):
    return inverse * (grad_hat - normed * lax.optimization_barrier(jnp.mean(grad_hat * normed, axis=-1, keepdims=True)))

def rotary_tables(places, width):
    half = width // 2
    freqs = ROPE_BASE ** (-(jnp.arange(half, dtype=jnp.float32) * 2.0) / width)
    angles = places.astype(jnp.float32)[:, None] * freqs[None, :]
    return (jnp.cos(angles), jnp.sin(angles))

def rotate(inputs, cosine, sine):
    half = inputs.shape[-1] // 2
    first = inputs[:, :half]
    second = inputs[:, half:]
    return jnp.concatenate([first * cosine - second * sine, second * cosine + first * sine], axis=-1)

def gelu_parts(inputs):
    inner = GELU_SCALE * (inputs + 0.044715 * inputs * inputs * inputs)
    tangent = jnp.tanh(inner)
    result = 0.5 * inputs * (1.0 + tangent)
    slope = 0.5 * (1.0 + tangent) + 0.5 * inputs * (1.0 - tangent * tangent) * GELU_SCALE * (1.0 + 3.0 * 0.044715 * inputs * inputs)
    return (result, slope)

def window_mask(segments):
    length = segments.shape[0]
    places = jnp.arange(length, dtype=jnp.int32)
    offset = places[:, None] - places[None, :]
    same = segments[:, None] == segments[None, :]
    return same & (offset >= 0) & (offset < WINDOW)

def contract_rows(left, right):
    return lax.dot_general(left, right, (((0,), (0,)), ((), ())), preferred_element_type=jnp.float32)

def contract_cols(left, right):
    return lax.dot_general(left, right, (((1,), (1,)), ((), ())), preferred_element_type=jnp.float32)

def attend_scores(queries, keys, allowed, scale):
    return jnp.where(allowed, contract_cols(queries, keys) * scale, MASKED)

def attend_forward(queries, keys, values, allowed, scale):
    scores = attend_scores(queries, keys, allowed, scale)
    top = lax.optimization_barrier(jnp.max(scores, axis=-1, keepdims=True))
    totals = lax.optimization_barrier(jnp.sum(jnp.exp(scores - top), axis=-1, keepdims=True))
    logsum = top + jnp.log(totals)
    probs = jnp.exp(scores - logsum).astype(jnp.bfloat16)
    return (jnp.dot(probs, values, preferred_element_type=jnp.float32), logsum)

def attend_backward(queries, keys, values, allowed, scale, logsum, grad_heads):
    probs = jnp.exp(attend_scores(queries, keys, allowed, scale) - logsum)
    grad_values = contract_rows(probs.astype(jnp.bfloat16), grad_heads)
    grad_probs = contract_cols(grad_heads, values)
    centre = lax.optimization_barrier(jnp.sum(probs * grad_probs, axis=-1, keepdims=True))
    grad_scores = (probs * (grad_probs - centre) * scale).astype(jnp.bfloat16)
    grad_queries = jnp.dot(grad_scores, keys, preferred_element_type=jnp.float32)
    grad_keys = contract_rows(grad_scores, queries)
    return (grad_queries, grad_keys, grad_values)

def layer_sequence(tokens, cotangent, segments, places, weights):
    w_query, w_key, w_value, w_out, w_gate, w_up, w_down = weights[:7]
    gain_in, gain_post, gain_ffw_in, gain_ffw_post, gain_query, gain_key = [g.astype(jnp.float32) for g in weights[7:]]
    width = w_key.shape[1]
    heads = w_query.shape[1] // width
    scale = 1.0 / math.sqrt(width)
    residual = tokens.astype(jnp.float32)
    normed_in, inverse_in = normalize(residual)
    attn_rows = (normed_in * gain_in).astype(jnp.bfloat16)
    cosine, sine = rotary_tables(places, width)
    allowed = window_mask(segments)
    key_hat, key_inverse = normalize(jnp.dot(attn_rows, w_key, preferred_element_type=jnp.float32))
    keys = rotate(key_hat * gain_key, cosine, sine).astype(jnp.bfloat16)
    values = jnp.dot(attn_rows, w_value, preferred_element_type=jnp.float32).astype(jnp.bfloat16)
    saved = []
    outputs = []
    for which in range(heads):
        columns = w_query[:, which * width:(which + 1) * width]
        query_hat, query_inverse = normalize(jnp.dot(attn_rows, columns, preferred_element_type=jnp.float32))
        queries = rotate(query_hat * gain_query, cosine, sine).astype(jnp.bfloat16)
        piece, logsum = attend_forward(queries, keys, values, allowed, scale)
        saved.append((query_hat, query_inverse, queries, logsum))
        outputs.append(piece)
    heads_out = jnp.concatenate(outputs, axis=1).astype(jnp.bfloat16)
    attn_sum = jnp.dot(heads_out, w_out, preferred_element_type=jnp.float32)
    attn_hat, attn_inverse = normalize(attn_sum)
    hidden = residual + attn_hat * gain_post
    mid_hat, mid_inverse = normalize(hidden)
    ffw_rows = (mid_hat * gain_ffw_in).astype(jnp.bfloat16)
    gate = jnp.dot(ffw_rows, w_gate, preferred_element_type=jnp.float32)
    upward = jnp.dot(ffw_rows, w_up, preferred_element_type=jnp.float32)
    gelu_value, gelu_slope = gelu_parts(gate)
    act = (gelu_value * upward).astype(jnp.bfloat16)
    ffw_sum = jnp.dot(act, w_down, preferred_element_type=jnp.float32)
    ffw_hat, ffw_inverse = normalize(ffw_sum)
    layer_out = (hidden + ffw_hat * gain_ffw_post).astype(jnp.bfloat16)
    grad_out = cotangent.astype(jnp.float32)
    grad_post_ffw = lax.optimization_barrier(jnp.sum(grad_out * ffw_hat, axis=0))
    grad_ffw = normalize_back(grad_out * gain_ffw_post, ffw_hat, ffw_inverse).astype(jnp.bfloat16)
    grad_down = contract_rows(act, grad_ffw)
    grad_act = contract_cols(grad_ffw, w_down)
    grad_gate_in = (grad_act * upward * gelu_slope).astype(jnp.bfloat16)
    grad_up_in = (grad_act * gelu_value).astype(jnp.bfloat16)
    grad_gate = contract_rows(ffw_rows, grad_gate_in)
    grad_up = contract_rows(ffw_rows, grad_up_in)
    grad_mid = contract_cols(grad_gate_in, w_gate) + contract_cols(grad_up_in, w_up)
    grad_pre_ffw = lax.optimization_barrier(jnp.sum(grad_mid * mid_hat, axis=0))
    grad_hidden = grad_out + normalize_back(grad_mid * gain_ffw_in, mid_hat, mid_inverse)
    grad_post_attn = lax.optimization_barrier(jnp.sum(grad_hidden * attn_hat, axis=0))
    grad_attn = normalize_back(grad_hidden * gain_post, attn_hat, attn_inverse).astype(jnp.bfloat16)
    grad_output = contract_rows(heads_out, grad_attn)
    grad_heads = contract_cols(grad_attn, w_out).astype(jnp.bfloat16)
    grad_query_norm = jnp.zeros((width,), jnp.float32)
    grad_key_norm = jnp.zeros((width,), jnp.float32)
    grad_key = jnp.zeros(w_key.shape, jnp.float32)
    grad_value = jnp.zeros(w_value.shape, jnp.float32)
    grad_in_rows = jnp.zeros(residual.shape, jnp.float32)
    query_blocks = []
    for which in range(heads):
        query_hat, query_inverse, queries, logsum = saved[which]
        head_grad = grad_heads[:, which * width:(which + 1) * width]
        grad_queries, grad_keys, grad_values = attend_backward(queries, keys, values, allowed, scale, logsum, head_grad)
        grad_query_turned = rotate(grad_queries, cosine, -sine)
        grad_query_norm = grad_query_norm + lax.optimization_barrier(jnp.sum(grad_query_turned * query_hat, axis=0))
        query_in = normalize_back(grad_query_turned * gain_query, query_hat, query_inverse).astype(jnp.bfloat16)
        grad_key_turned = rotate(grad_keys, cosine, -sine)
        grad_key_norm = grad_key_norm + lax.optimization_barrier(jnp.sum(grad_key_turned * key_hat, axis=0))
        key_in = normalize_back(grad_key_turned * gain_key, key_hat, key_inverse).astype(jnp.bfloat16)
        value_in = grad_values.astype(jnp.bfloat16)
        query_blocks.append(contract_rows(attn_rows, query_in))
        grad_key = grad_key + contract_rows(attn_rows, key_in)
        grad_value = grad_value + contract_rows(attn_rows, value_in)
        columns = w_query[:, which * width:(which + 1) * width]
        grad_in_rows = grad_in_rows + contract_cols(query_in, columns) + contract_cols(key_in, w_key) + contract_cols(value_in, w_value)
    grad_query = jnp.concatenate(query_blocks, axis=1)
    grad_pre_attn = lax.optimization_barrier(jnp.sum(grad_in_rows * normed_in, axis=0))
    grad_tokens = grad_hidden + normalize_back(grad_in_rows * gain_in, normed_in, inverse_in)
    grads = (grad_query, grad_key, grad_value, grad_output, grad_gate, grad_up, grad_down, grad_pre_attn, grad_post_attn, grad_pre_ffw, grad_post_ffw, grad_query_norm, grad_key_norm)
    return (layer_out, grad_tokens, grads)

def reference(tokens, cotangent, segment_ids, positions, w_query, w_key, w_value, w_out, w_gate, w_up, w_down, prenorm_attn, postnorm_attn, prenorm_ffw, postnorm_ffw, query_norm, key_norm):
    weights = (w_query, w_key, w_value, w_out, w_gate, w_up, w_down, prenorm_attn, postnorm_attn, prenorm_ffw, postnorm_ffw, query_norm, key_norm)
    count = segment_ids.shape[0]
    length = segment_ids.shape[1]
    model_width = tokens.shape[1]
    zeros = tuple((jnp.zeros(weight.shape, jnp.float32) for weight in weights))

    def step(carry, inputs):
        token_rows, cotangent_rows, segments, places = inputs
        result, grad_rows, grads = layer_sequence(token_rows, cotangent_rows, segments, places, weights)
        return (tuple((total + grad for total, grad in zip(carry, grads))), (result, grad_rows))
    totals, (results, grad_rows) = lax.scan(step, zeros, (tokens.reshape(count, length, model_width), cotangent.reshape(count, length, model_width), segment_ids, positions))
    return (results.reshape(count * length, model_width), grad_rows.reshape(count * length, model_width), totals[0], totals[1], totals[2], totals[3], totals[4], totals[5], totals[6], totals[7], totals[8], totals[9], totals[10], totals[11], totals[12])
```

```python
import functools
import math

import jax
import jax.numpy as jnp
from jax import lax
from jax.experimental import pallas as pl
from jax.experimental.pallas import tpu as pltpu
from jax.sharding import PartitionSpec as P

WINDOW = 512
EPSILON = 1e-06
ROPE_BASE = 10000.0
GELU_SCALE = math.sqrt(2.0 / math.pi)
MASKED = -1e30
BF16 = jnp.bfloat16
F32 = jnp.float32
ROWS = 160
WIDTH = 1152
CHUNK = 72
FFPAD = 1792
ATTN_COLS = 1280
MESH = pl.DeviceIdType.MESH


def normalize(inputs):
    inverse = lax.rsqrt(jnp.mean(inputs * inputs, axis=-1, keepdims=True) + EPSILON)
    return (inputs * inverse, inverse)


def normalize_back(grad_hat, normed, inverse):
    return inverse * (grad_hat - normed * jnp.mean(grad_hat * normed, axis=-1, keepdims=True))


def rotary_tables(places, width):
    half = width // 2
    freqs = ROPE_BASE ** (-(jnp.arange(half, dtype=jnp.float32) * 2.0) / width)
    angles = places.astype(jnp.float32)[:, None] * freqs[None, :]
    return (jnp.cos(angles), jnp.sin(angles))


def rotate(inputs, cosine, sine):
    half = inputs.shape[-1] // 2
    first = inputs[:, :half]
    second = inputs[:, half:]
    return jnp.concatenate(
        [first * cosine - second * sine, second * cosine + first * sine], axis=-1
    )


def gelu_parts(inputs):
    inner = GELU_SCALE * (inputs + 0.044715 * inputs * inputs * inputs)
    tangent = jnp.tanh(inner)
    result = 0.5 * inputs * (1.0 + tangent)
    slope = 0.5 * (1.0 + tangent) + 0.5 * inputs * (1.0 - tangent * tangent) * GELU_SCALE * (
        1.0 + 3.0 * 0.044715 * inputs * inputs
    )
    return (result, slope)


def window_mask(segments):
    length = segments.shape[0]
    places = jnp.arange(length, dtype=jnp.int32)
    offset = places[:, None] - places[None, :]
    same = segments[:, None] == segments[None, :]
    return same & (offset >= 0) & (offset < WINDOW)


def contract_rows(left, right):
    return lax.dot_general(
        left, right, (((0,), (0,)), ((), ())), preferred_element_type=jnp.float32
    )


def contract_cols(left, right):
    return lax.dot_general(
        left, right, (((1,), (1,)), ((), ())), preferred_element_type=jnp.float32
    )


def attend_scores(queries, keys, allowed, scale):
    return jnp.where(allowed, contract_cols(queries, keys) * scale, MASKED)


def attend_forward(queries, keys, values, allowed, scale):
    scores = attend_scores(queries, keys, allowed, scale)
    top = jnp.max(scores, axis=-1, keepdims=True)
    totals = jnp.sum(jnp.exp(scores - top), axis=-1, keepdims=True)
    logsum = top + jnp.log(totals)
    probs = jnp.exp(scores - logsum).astype(jnp.bfloat16)
    return (jnp.dot(probs, values, preferred_element_type=jnp.float32), logsum)


def attend_backward(queries, keys, values, allowed, scale, logsum, grad_heads):
    probs = jnp.exp(attend_scores(queries, keys, allowed, scale) - logsum)
    grad_values = contract_rows(probs.astype(jnp.bfloat16), grad_heads)
    grad_probs = contract_cols(grad_heads, values)
    centre = jnp.sum(probs * grad_probs, axis=-1, keepdims=True)
    grad_scores = (probs * (grad_probs - centre) * scale).astype(jnp.bfloat16)
    grad_queries = jnp.dot(grad_scores, keys, preferred_element_type=jnp.float32)
    grad_keys = contract_rows(grad_scores, queries)
    return (grad_queries, grad_keys, grad_values)


def wrap(value):
    return lax.rem(value + 8, 4)


class Place:
    def __init__(self):
        dp = lax.axis_index("dp")
        self.z = lax.axis_index("tensor")
        self.core = lax.rem(dp, 2)
        self.x = lax.rem(dp // 2, 4)
        self.y = dp // 8
        self.s = 1 - 2 * self.core

    def device(self, y=None, x=None, core=None, z=None):
        y = self.y if y is None else y
        x = self.x if x is None else x
        core = self.core if core is None else core
        z = self.z if z is None else z
        return ((y * 4 + x) * 2 + core, z)

    def partner(self):
        return self.device(core=1 - self.core)

    def greet(self, xy, far_z=False):
        barrier = pltpu.get_barrier_semaphore()
        others = [self.device(z=wrap(self.z + 1)), self.device(z=wrap(self.z - 1))]
        if xy:
            others += [
                self.partner(),
                self.device(x=wrap(self.x + 1)),
                self.device(x=wrap(self.x - 1)),
                self.device(y=wrap(self.y + 1)),
                self.device(y=wrap(self.y - 1)),
            ]
        if far_z:
            others.append(self.device(z=wrap(self.z + 2)))
        for other in others:
            pl.semaphore_signal(barrier, inc=1, device_id=other, device_id_type=MESH)
        pl.semaphore_wait(barrier, len(others))


def remote(src, dst, send, recv, device):
    return pltpu.make_async_remote_copy(
        src_ref=src,
        dst_ref=dst,
        send_sem=send,
        recv_sem=recv,
        device_id=device,
        device_id_type=MESH,
    )


def run_streams(streams):
    streams = list(streams)
    while streams:
        alive = []
        for stream in streams:
            try:
                next(stream)
                alive.append(stream)
            except StopIteration:
                pass
        streams = alive


def halves(n):
    tiles = n // 256
    a = (tiles + 1) // 2
    return (a * 128, (tiles - a) * 128)


class Axes:
    def __init__(self, place, which, n):
        wa, wb = halves(n)
        self.which = which
        self.w = wa if which == 0 else wb
        start = 0 if which == 0 else wa
        self.place = place
        self.mine = pl.ds(pl.multiple_of(place.core * (n // 2) + start, 128), self.w)
        self.theirs = pl.ds(pl.multiple_of((1 - place.core) * (n // 2) + start, 128), self.w)
        self.u, self.v = (place.x, place.y) if which == 0 else (place.y, place.x)

    def device(self, u=None, v=None):
        u = self.u if u is None else u
        v = self.v if v is None else v
        return self.place.device(y=v, x=u) if self.which == 0 else self.place.device(y=u, x=v)

    def chunk(self, ref, u, v, cols):
        return ref.at[v, u, :, cols] if self.which == 0 else ref.at[u, v, :, cols]

    def group(self, ref, v, cols):
        return ref.at[v, :, :, cols] if self.which == 0 else ref.at[:, v, :, cols]


def merge_own(place, own, other, both, send, recv):
    copy = remote(own, other, send, recv, place.partner())
    copy.start()
    yield
    copy.wait()
    mine = own[...].astype(F32)
    theirs = other[...].astype(F32)
    first = place.core == 0
    both[...] = jnp.concatenate(
        [jnp.where(first, mine, theirs), jnp.where(first, theirs, mine)], axis=0
    ).astype(BF16)


def gather_half(ax, both, out, ring_send, ring_recv, chip_send, chip_recv):
    place, s = ax.place, ax.place.s
    cols = ax.mine
    sent = []

    def send(src, u, v, device, k):
        copy = remote(src, ax.chunk(out, u, v, cols), ring_send.at[k], ring_recv.at[k], device)
        copy.start()
        sent.append(copy)

    def arrive(u, v, k):
        here = ax.chunk(out, u, v, cols)
        remote(here, here, ring_send.at[k], ring_recv.at[k], place.partner()).wait_recv()
        copy = remote(here, here, chip_send.at[k], chip_recv.at[k], place.partner())
        copy.start()
        sent.append(copy)

    def along_v(src, u, r):
        send(src, u, ax.v, ax.device(v=wrap(ax.v + s)), 3 + 3 * r)
        send(src, u, ax.v, ax.device(v=wrap(ax.v - s)), 4 + 3 * r)

    own = both.at[:, cols]
    us = [ax.u, wrap(ax.u - s), wrap(ax.u + s), wrap(ax.u + 2)]
    send(own, ax.u, ax.v, ax.device(u=wrap(ax.u + s)), 0)
    send(own, ax.u, ax.v, ax.device(u=wrap(ax.u - s)), 1)
    along_v(own, ax.u, 0)
    yield
    arrive(us[1], ax.v, 0)
    src = ax.chunk(out, us[1], ax.v, cols)
    send(src, us[1], ax.v, ax.device(u=wrap(ax.u + s)), 2)
    along_v(src, us[1], 1)
    yield
    arrive(us[2], ax.v, 1)
    along_v(ax.chunk(out, us[2], ax.v, cols), us[2], 2)
    yield
    for r in range(4):
        if r == 1:
            arrive(us[3], ax.v, 2)
            along_v(ax.chunk(out, us[3], ax.v, cols), us[3], 3)
            yield
        v = wrap(ax.v - s)
        arrive(us[r], v, 3 + 3 * r)
        send(ax.chunk(out, us[r], v, cols), us[r], v, ax.device(v=wrap(ax.v + s)), 5 + 3 * r)
        yield
        arrive(us[r], wrap(ax.v + s), 4 + 3 * r)
        yield
    for r in range(4):
        arrive(us[r], wrap(ax.v + 2), 5 + 3 * r)
        yield
    for copy in sent:
        copy.wait_send()
    yield
    theirs = [ax.u, wrap(ax.u + s), wrap(ax.u - s), wrap(ax.u + 2)]
    landing = [(theirs[1], ax.v), (theirs[2], ax.v), (theirs[3], ax.v)]
    for r in range(4):
        landing += [(theirs[r], wrap(ax.v + s)), (theirs[r], wrap(ax.v - s)), (theirs[r], wrap(ax.v + 2))]
    for k, (u, v) in enumerate(landing):
        here = ax.chunk(out, u, v, ax.theirs)
        remote(here, here, chip_send.at[k], chip_recv.at[k], place.partner()).wait_recv()


def gather_stream(place, own, out, scratch):
    other, both, sems, local = scratch
    n = own.shape[1]
    yield from merge_own(place, own, other, both, sems.at[0, 0, 0, 15], sems.at[0, 0, 1, 15])
    keep = pltpu.make_async_copy(both, out.at[place.y, place.x], local)
    keep.start()
    parts = [
        gather_half(
            Axes(place, h, n), both, out, sems.at[h, 0, 0], sems.at[h, 0, 1], sems.at[h, 1, 0], sems.at[h, 1, 1]
        )
        for h in (0, 1)
    ]
    while parts:
        alive = []
        for part in parts:
            try:
                next(part)
                alive.append(part)
            except StopIteration:
                pass
        parts = alive
        yield
    keep.wait()


def gather_scratch(n):
    return [
        pltpu.VMEM((36, n), BF16),
        pltpu.VMEM((CHUNK, n), BF16),
        pltpu.SemaphoreType.DMA((2, 2, 2, 16)),
        pltpu.SemaphoreType.DMA,
    ]


def add_chunks(count, target, *terms):
    def body(i, carry):
        total = terms[0](i)[...].astype(F32)
        for term in terms[1:]:
            total = total + term(i)[...].astype(F32)
        target(i)[...] = total.astype(BF16)
        return carry

    if count == 1:
        body(0, 0)
    else:
        lax.fori_loop(0, count, body, 0)


def scatter_half(ax, grads, final, bufs, sems):
    held, got, b1, b2, b3, c1, c2, c3, total = bufs
    place, s = ax.place, ax.place.s
    vs = [wrap(ax.v + 2), wrap(ax.v - s), wrap(ax.v + s), ax.v]
    for_partner = [wrap(ax.v + 2), wrap(ax.v + s), wrap(ax.v - s), ax.v]
    sent, loads, gets = [], [], []
    for k in range(4):
        give = remote(
            ax.group(grads, for_partner[k], ax.theirs),
            got.at[k],
            sems.at[0, k],
            sems.at[1, k],
            place.partner(),
        )
        give.start()
        sent.append(give)
        gets.append(give)
        load = pltpu.make_async_copy(ax.group(grads, vs[k], ax.mine), held.at[k], sems.at[2, k])
        load.start()
        loads.append(load)
    yield

    def chip_sum(k):
        loads[k].wait()
        gets[k].wait_recv()
        add_chunks(4, lambda i: got.at[k, i], lambda i: got.at[k, i], lambda i: held.at[k, i])

    def send(src, dst, k, device):
        copy = remote(src, dst, sems.at[0, k], sems.at[1, k], device)
        copy.start()
        sent.append(copy)
        return copy

    chip_sum(0)
    far = send(got.at[0], b1, 4, ax.device(v=wrap(ax.v + s)))
    yield
    chip_sum(1)
    back = send(got.at[1], b2, 5, ax.device(v=wrap(ax.v - s)))
    yield
    chip_sum(2)
    yield
    far.wait_recv()
    add_chunks(4, lambda i: b1.at[i], lambda i: b1.at[i], lambda i: got.at[2, i])
    forth = send(b1, b3, 6, ax.device(v=wrap(ax.v + s)))
    yield
    loads[3].wait()
    gets[3].wait_recv()
    back.wait_recv()
    yield
    forth.wait_recv()
    add_chunks(
        4,
        lambda i: total.at[i],
        lambda i: got.at[3, i],
        lambda i: held.at[3, i],
        lambda i: b2.at[i],
        lambda i: b3.at[i],
    )
    far = send(total.at[wrap(ax.u + 2)], c1, 7, ax.device(u=wrap(ax.u + s)))
    back = send(total.at[wrap(ax.u - s)], c2, 8, ax.device(u=wrap(ax.u - s)))
    yield
    far.wait_recv()
    add_chunks(1, lambda i: c1, lambda i: c1, lambda i: total.at[wrap(ax.u + s)])
    forth = send(c1, c3, 9, ax.device(u=wrap(ax.u + s)))
    yield
    back.wait_recv()
    forth.wait_recv()
    add_chunks(1, lambda i: c2, lambda i: total.at[ax.u], lambda i: c2, lambda i: c3)
    keep = pltpu.make_async_copy(c2, final.at[:, ax.mine], sems.at[2, 4])
    keep.start()
    last = send(c2, final.at[:, ax.mine], 10, place.partner())
    yield
    for copy in sent:
        copy.wait_send()
    keep.wait()
    remote(c2, final.at[:, ax.theirs], sems.at[0, 10], sems.at[1, 10], place.partner()).wait_recv()


def scatter_scratch(n):
    shapes = []
    for w in halves(n):
        shapes += [pltpu.VMEM((4, 4, CHUNK, w), BF16)] * 2
        shapes += [pltpu.VMEM((4, CHUNK, w), BF16)] * 3
        shapes += [pltpu.VMEM((CHUNK, w), BF16)] * 3
        shapes += [pltpu.VMEM((4, CHUNK, w), BF16)]
        shapes += [pltpu.SemaphoreType.DMA((3, 11))]
    return shapes


def scatter_streams(place, grads, final, scratch):
    n = grads.shape[3]
    for h in (0, 1):
        part = scratch[10 * h : 10 * h + 10]
        yield scatter_half(Axes(place, h, n), grads, final, part[:9], part[9])


def rows_gather(place, out, sems):
    s, z = place.s, place.z
    ahead, behind = place.device(z=wrap(z + s)), place.device(z=wrap(z - s))

    def copy(slot, k, device):
        return remote(out.at[slot], out.at[slot], sems.at[0, k], sems.at[1, k], device)

    first = copy(z, 0, ahead)
    first.start()
    second = copy(z, 1, behind)
    second.start()
    yield
    copy(wrap(z - s), 0, ahead).wait_recv()
    relay = copy(wrap(z - s), 2, ahead)
    relay.start()
    yield
    copy(wrap(z + s), 1, ahead).wait_recv()
    yield
    yield
    copy(wrap(z + 2), 2, ahead).wait_recv()
    for sent in (first, second, relay):
        sent.wait_send()


def rows_scatter(place, parts, bufs, sems):
    s, z = place.s, place.z
    b1, b2, b3 = bufs
    ahead, behind = place.device(z=wrap(z + s)), place.device(z=wrap(z - s))

    def copy(src, dst, k, device):
        return remote(src, dst, sems.at[0, k], sems.at[1, k], device)

    far = copy(parts.at[wrap(z + 2)], b1, 0, ahead)
    far.start()
    back = copy(parts.at[wrap(z - s)], b2, 1, behind)
    back.start()
    yield
    yield
    far.wait_recv()
    mid = wrap(z + s)

    def body(i, carry):
        rows = pl.ds(pl.multiple_of(i * 32, 32), 32)
        b1[rows, :] = (b1[rows, :].astype(F32) + parts[mid, rows, :].astype(F32)).astype(BF16)
        return carry

    lax.fori_loop(0, ROWS // 32, body, 0)
    forth = copy(b1, b3, 2, ahead)
    forth.start()
    yield
    back.wait_recv()
    yield
    forth.wait_recv()
    for sent in (far, back, forth):
        sent.wait_send()


def rows_scratch():
    return [pltpu.VMEM((ROWS, WIDTH), BF16)] * 3 + [pltpu.SemaphoreType.DMA((2, 3))] * 2


def row_blocks(body):
    def step(i, carry):
        body(pl.ds(pl.multiple_of(i * 16, 16), 16))
        return carry

    lax.fori_loop(0, ROWS // 16, step, 0)


def col_sum(ref, row, values):
    ref[8 * row : 8 * row + 8, :] = ref[8 * row : 8 * row + 8, :] + values[:8] + values[8:]


def start_kernel(tokens, attn_own, rows_out, mats_out, sems, *scratch):
    place = Place()
    place.greet(True)

    def z_stream():
        rows_out[place.z] = tokens[...]
        yield from rows_gather(place, rows_out, sems)

    run_streams([gather_stream(place, attn_own, mats_out, scratch), z_stream()])


def middle_kernel(parts, tokens, gains, own_g, own_u, own_d, rows_out, attn_sum, full_g, full_u, full_d, *scratch):
    place = Place()
    place.greet(True)
    b1, b2, b3, sems, sems2 = scratch[:5]

    def z_stream():
        yield from rows_scatter(place, parts, (b1, b2, b3), sems)

        def body(rows):
            total = (
                parts[place.z, rows, :].astype(F32) + b2[rows, :].astype(F32) + b3[rows, :].astype(F32)
            )
            attn_sum[rows, :] = total
            hat, _ = normalize(total)
            hidden = tokens[rows, :].astype(F32) + hat * gains[1:2, :]
            mid, _ = normalize(hidden)
            rows_out[place.z, rows, :] = (mid * gains[2:3, :]).astype(BF16)

        row_blocks(body)
        yield from rows_gather(place, rows_out, sems2)

    run_streams(
        [
            z_stream(),
            gather_stream(place, own_g, full_g, scratch[5:9]),
            gather_stream(place, own_u, full_u, scratch[9:13]),
            gather_stream(place, own_d, full_d, scratch[13:17]),
        ]
    )


def turn_kernel(parts, tokens, attn_sum, gains, cotangent, rows_out, layer_out, sums, *scratch):
    place = Place()
    place.greet(False)
    b1, b2, b3, sems, sems2 = scratch[:5]
    sums[...] = jnp.zeros_like(sums)

    def z_stream():
        yield from rows_scatter(place, parts, (b1, b2, b3), sems)

        def body(rows):
            total = (
                parts[place.z, rows, :].astype(F32) + b2[rows, :].astype(F32) + b3[rows, :].astype(F32)
            )
            attn_hat, _ = normalize(attn_sum[rows, :])
            hidden = tokens[rows, :].astype(F32) + attn_hat * gains[1:2, :]
            hat, inverse = normalize(total)
            layer_out[rows, :] = (hidden + hat * gains[3:4, :]).astype(BF16)
            grad = cotangent[rows, :].astype(F32)
            col_sum(sums, 0, grad * hat)
            rows_out[place.z, rows, :] = normalize_back(grad * gains[3:4, :], hat, inverse).astype(BF16)

        row_blocks(body)
        yield from rows_gather(place, rows_out, sems2)

    run_streams([z_stream()])


def back_kernel(
    parts, tokens, attn_sum, gains, cotangent, grad_g, grad_u, grad_d,
    rows_out, grad_hidden, sums, sum_g, sum_u, sum_d, *scratch
):
    place = Place()
    place.greet(True)
    b1, b2, b3, sems, sems2 = scratch[:5]
    sums[...] = jnp.zeros_like(sums)

    def z_stream():
        yield from rows_scatter(place, parts, (b1, b2, b3), sems)

        def body(rows):
            grad_mid = (
                parts[place.z, rows, :].astype(F32) + b2[rows, :].astype(F32) + b3[rows, :].astype(F32)
            )
            attn_hat, attn_inverse = normalize(attn_sum[rows, :])
            hidden = tokens[rows, :].astype(F32) + attn_hat * gains[1:2, :]
            mid, inverse = normalize(hidden)
            col_sum(sums, 0, grad_mid * mid)
            grad = cotangent[rows, :].astype(F32) + normalize_back(grad_mid * gains[2:3, :], mid, inverse)
            grad_hidden[rows, :] = grad
            col_sum(sums, 1, grad * attn_hat)
            rows_out[place.z, rows, :] = normalize_back(
                grad * gains[1:2, :], attn_hat, attn_inverse
            ).astype(BF16)

        row_blocks(body)
        yield from rows_gather(place, rows_out, sems2)

    streams = [z_stream()]
    for i, (grads, final) in enumerate(((grad_d, sum_d), (grad_g, sum_g), (grad_u, sum_u))):
        streams += list(scatter_streams(place, grads, final, scratch[5 + 20 * i : 25 + 20 * i]))
    run_streams(streams)


def end_kernel(parts, grads, grad_rows, final, shared, *scratch):
    place = Place()
    place.greet(True, far_z=True)
    b1, b2, b3, sems, sems2 = scratch[:5]
    got, zsend, zrecv = scratch[5:8]

    def z_stream():
        yield from rows_scatter(place, parts, (b1, b2, b3), sems)

        def body(rows):
            grad_rows[rows, :] = (
                parts[place.z, rows, :].astype(F32) + b2[rows, :].astype(F32) + b3[rows, :].astype(F32)
            )

        row_blocks(body)

    run_streams([z_stream()] + list(scatter_streams(place, grads, final, scratch[8:28])))
    cols = pl.ds(512, 768)
    copies = []
    for k in range(3):
        copy = remote(
            final.at[:, cols], got.at[k], zsend.at[k], zrecv.at[k], place.device(z=wrap(place.z + k + 1))
        )
        copy.start()
        copies.append(copy)
    for copy in copies:
        copy.wait()
    total = final[:, cols].astype(F32)
    for k in range(3):
        total = total + got[k].astype(F32)
    shared[...] = total


def call(kernel, outs, ins, spaces, out_spaces, scratch, ident):
    return pl.pallas_call(
        kernel,
        out_shape=[jax.ShapeDtypeStruct(shape, dtype) for shape, dtype in outs],
        in_specs=[pl.BlockSpec(memory_space=space) for space in spaces],
        out_specs=[pl.BlockSpec(memory_space=space) for space in out_spaces],
        scratch_shapes=scratch,
        compiler_params=pltpu.CompilerParams(
            collective_id=ident, has_side_effects=True, vmem_limit_bytes=60 * 1024 * 1024
        ),
        name=kernel.__name__,
    )(*ins)


def local(
    tokens,
    cotangent,
    segment_ids,
    positions,
    w_query,
    w_key,
    w_value,
    w_out,
    w_gate,
    w_up,
    w_down,
    prenorm_attn,
    postnorm_attn,
    prenorm_ffw,
    postnorm_ffw,
    query_norm,
    key_norm,
):
    vm, hbm = pltpu.VMEM, pl.ANY
    shard = 36
    core = lax.rem(lax.axis_index("dp"), 2)
    hidden_units = w_gate.shape[1]
    pad = ((0, 0), (0, FFPAD - hidden_units))
    width = w_key.shape[1]

    def column(vector):
        return jnp.pad(vector, (0, shard - vector.shape[0]))[:, None]

    attn_own = jnp.concatenate(
        [w_query, w_out.T, w_key, w_value]
        + [column(g) for g in (prenorm_attn, postnorm_attn, prenorm_ffw, postnorm_ffw, query_norm, key_norm)]
        + [jnp.zeros((shard, ATTN_COLS - 1024 - 6), BF16)],
        axis=1,
    )
    tokens_all, mats = call(
        start_kernel,
        [((4, ROWS, WIDTH), BF16), ((4, 4, CHUNK, ATTN_COLS), BF16)],
        [tokens, attn_own],
        [vm, vm],
        [vm, hbm],
        [pltpu.SemaphoreType.DMA((2, 3))] + gather_scratch(ATTN_COLS),
        0,
    )
    mats = mats.reshape(WIDTH, ATTN_COLS)
    full_query, full_out = mats[:, :256], mats[:, 256:512]
    full_key, full_value = mats[:, 512:768], mats[:, 768:1024]
    small = mats[:, 1024:1032].astype(F32).T
    gains = small
    gain_in = small[0]
    gain_query = small[4].reshape(32, shard)[:, :8].reshape(-1)
    gain_key = small[5].reshape(32, shard)[:, :8].reshape(-1)
    normed_all, _ = normalize(tokens_all.reshape(4 * ROWS, WIDTH).astype(F32))
    attn_rows = (normed_all * gain_in).astype(BF16)
    scale = 1.0 / math.sqrt(width)
    cosine, sine = rotary_tables(positions.reshape(-1), width)
    mask = window_mask(segment_ids[0])
    key_hat, key_inverse = normalize(jnp.dot(attn_rows, full_key, preferred_element_type=F32))
    keys = rotate(key_hat * gain_key, cosine, sine).astype(BF16)
    values = jnp.dot(attn_rows, full_value, preferred_element_type=F32).astype(BF16)
    query_hat, query_inverse = normalize(jnp.dot(attn_rows, full_query, preferred_element_type=F32))
    queries = rotate(query_hat * gain_query, cosine, sine).astype(BF16)
    piece, logsum = attend_forward(queries, keys, values, mask, scale)
    heads_out = piece.astype(BF16)
    attn_part = contract_cols(heads_out, full_out).astype(BF16)
    whole = ((4, 4, CHUNK, FFPAD), BF16)
    ffw_rows, attn_sum, full_gate, full_up, full_down = call(
        middle_kernel,
        [((4, ROWS, WIDTH), BF16), ((ROWS, WIDTH), F32), whole, whole, whole],
        [
            attn_part.reshape(4, ROWS, WIDTH),
            tokens,
            gains,
            jnp.pad(w_gate, pad),
            jnp.pad(w_up, pad),
            jnp.pad(w_down.T, pad),
        ],
        [vm] * 6,
        [vm, vm, hbm, hbm, hbm],
        rows_scratch() + gather_scratch(FFPAD) * 3,
        1,
    )
    ffw_rows = ffw_rows.reshape(4 * ROWS, WIDTH)
    full_gate = full_gate.reshape(WIDTH, FFPAD)
    full_up = full_up.reshape(WIDTH, FFPAD)
    full_down = full_down.reshape(WIDTH, FFPAD)
    gate = jnp.dot(ffw_rows, full_gate, preferred_element_type=F32)
    upward = jnp.dot(ffw_rows, full_up, preferred_element_type=F32)
    gelu_value, gelu_slope = gelu_parts(gate)
    act = (gelu_value * upward).astype(BF16)
    ffw_part = contract_cols(act, full_down).astype(BF16)
    grad_ffw, layer_out, ffw_sums = call(
        turn_kernel,
        [((4, ROWS, WIDTH), BF16), ((ROWS, WIDTH), BF16), ((8, WIDTH), F32)],
        [ffw_part.reshape(4, ROWS, WIDTH), tokens, attn_sum, gains, cotangent],
        [vm] * 5,
        [vm] * 3,
        rows_scratch(),
        2,
    )
    grad_ffw = grad_ffw.reshape(4 * ROWS, WIDTH)
    grad_down = contract_rows(grad_ffw, act).astype(BF16)
    grad_act = jnp.dot(grad_ffw, full_down, preferred_element_type=F32)
    grad_gate_in = (grad_act * upward * gelu_slope).astype(BF16)
    grad_up_in = (grad_act * gelu_value).astype(BF16)
    grad_gate = contract_rows(ffw_rows, grad_gate_in).astype(BF16)
    grad_up = contract_rows(ffw_rows, grad_up_in).astype(BF16)
    mid_part = (contract_cols(grad_gate_in, full_gate) + contract_cols(grad_up_in, full_up)).astype(BF16)
    split = (4, 4, CHUNK, FFPAD)
    final = ((CHUNK, FFPAD), BF16)
    grad_attn, grad_hidden, mid_sums, sum_gate, sum_up, sum_down = call(
        back_kernel,
        [((4, ROWS, WIDTH), BF16), ((ROWS, WIDTH), F32), ((16, WIDTH), F32), final, final, final],
        [
            mid_part.reshape(4, ROWS, WIDTH),
            tokens,
            attn_sum,
            gains,
            cotangent,
            grad_gate.reshape(split),
            grad_up.reshape(split),
            grad_down.reshape(split),
        ],
        [vm] * 5 + [hbm] * 3,
        [vm] * 6,
        rows_scratch() + scatter_scratch(FFPAD) * 3,
        3,
    )
    grad_attn = grad_attn.reshape(4 * ROWS, WIDTH)
    grad_output = contract_rows(grad_attn, heads_out)
    grad_heads = jnp.dot(grad_attn, full_out, preferred_element_type=F32).astype(BF16)
    grad_queries, grad_keys, grad_values = attend_backward(
        queries, keys, values, mask, scale, logsum, grad_heads
    )
    grad_query_turned = rotate(grad_queries, cosine, -sine)
    grad_query_norm = jnp.sum(grad_query_turned * query_hat, axis=0)
    query_in = normalize_back(grad_query_turned * gain_query, query_hat, query_inverse).astype(BF16)
    grad_key_turned = rotate(grad_keys, cosine, -sine)
    grad_key_norm = jnp.sum(grad_key_turned * key_hat, axis=0)
    key_in = normalize_back(grad_key_turned * gain_key, key_hat, key_inverse).astype(BF16)
    value_in = grad_values.astype(BF16)
    grad_query = contract_rows(attn_rows, query_in)
    grad_key = contract_rows(attn_rows, key_in)
    grad_value = contract_rows(attn_rows, value_in)
    in_part = contract_cols(query_in, full_query)
    in_part = in_part + contract_cols(key_in, full_key)
    in_part = in_part + contract_cols(value_in, full_value)
    grad_pre_attn = jnp.sum(in_part * normed_all, axis=0)

    def placed_rows(vector):
        return jnp.pad(vector.reshape(32, 8), ((0, 0), (0, shard - 8))).reshape(-1)

    vectors = jnp.stack(
        [
            grad_pre_attn,
            jnp.sum(mid_sums[8:], axis=0),
            jnp.sum(mid_sums[:8], axis=0),
            jnp.sum(ffw_sums, axis=0),
            placed_rows(grad_query_norm),
            placed_rows(grad_key_norm),
        ]
    )
    small_grads = jnp.pad(vectors, ((0, ATTN_COLS - 1024 - 6), (0, 0))).T
    grads = jnp.concatenate(
        [g.astype(BF16) for g in (grad_query, grad_output, grad_key, grad_value, small_grads)], axis=1
    )
    grad_in_rows, sum_attn, sum_shared = call(
        end_kernel,
        [((ROWS, WIDTH), F32), ((CHUNK, ATTN_COLS), BF16), ((CHUNK, ATTN_COLS - 512), F32)],
        [in_part.astype(BF16).reshape(4, ROWS, WIDTH), grads.reshape(4, 4, CHUNK, ATTN_COLS)],
        [vm, hbm],
        [vm] * 3,
        rows_scratch()
        + [
            pltpu.VMEM((3, CHUNK, ATTN_COLS - 512), BF16),
            pltpu.SemaphoreType.DMA((3,)),
            pltpu.SemaphoreType.DMA((3,)),
        ]
        + scatter_scratch(ATTN_COLS),
        4,
    )
    normed_in, inverse_in = normalize(tokens.astype(F32))
    grad_tokens = grad_hidden + normalize_back(grad_in_rows * gain_in, normed_in, inverse_in)

    def own_rows(array):
        first = core == 0
        return jnp.where(first, array[:shard], array[shard:]).astype(F32)

    own_attn = own_rows(sum_attn[:, :512])
    own_shared = own_rows(sum_shared)
    own_small = own_shared[:, 512:520]
    return (
        layer_out,
        grad_tokens,
        own_attn[:, :256],
        own_shared[:, :256],
        own_shared[:, 256:512],
        own_attn[:, 256:].T,
        own_rows(sum_gate)[:, :hidden_units],
        own_rows(sum_up)[:, :hidden_units],
        own_rows(sum_down)[:, :hidden_units].T,
        own_small[:, 0],
        own_small[:, 1],
        own_small[:, 2],
        own_small[:, 3],
        own_small[:8, 4],
        own_small[:8, 5],
    )


def solution(mesh):
    placed = (
        P(("dp", "tensor"), None),
        P(("dp", "tensor"), None),
        P("dp", None),
        P("dp", None),
        P("dp", "tensor"),
        P("dp", None),
        P("dp", None),
        P("tensor", "dp"),
        P("dp", "tensor"),
        P("dp", "tensor"),
        P("tensor", "dp"),
        P("dp"),
        P("dp"),
        P("dp"),
        P("dp"),
        P("dp"),
        P("dp"),
    )
    return jax.shard_map(
        local,
        mesh=mesh,
        in_specs=placed,
        out_specs=(
            P(("dp", "tensor"), None),
            P(("dp", "tensor"), None),
            P("dp", "tensor"),
            P("dp", None),
            P("dp", None),
            P("tensor", "dp"),
            P("dp", "tensor"),
            P("dp", "tensor"),
            P("tensor", "dp"),
            P("dp"),
            P("dp"),
            P("dp"),
            P("dp"),
            P("dp"),
            P("dp"),
        ),
        check_vma=False,
    )
```

```python
import functools
import math

import jax
import jax.numpy as jnp
from jax import lax
from jax.experimental import pallas as pl
from jax.experimental.pallas import tpu as pltpu
from jax.sharding import PartitionSpec as P

WINDOW = 512
EPSILON = 1e-06
ROPE_BASE = 10000.0
GELU_SCALE = math.sqrt(2.0 / math.pi)
MASKED = -1e30
BF16 = jnp.bfloat16
F32 = jnp.float32
ROWS = 160
WIDTH = 1152
CHUNK = 72
FFPAD = 1792
ATTN_COLS = 1280
MESH = pl.DeviceIdType.MESH


def normalize(inputs):
    inverse = lax.rsqrt(jnp.mean(inputs * inputs, axis=-1, keepdims=True) + EPSILON)
    return (inputs * inverse, inverse)


def normalize_back(grad_hat, normed, inverse):
    return inverse * (grad_hat - normed * jnp.mean(grad_hat * normed, axis=-1, keepdims=True))


def rotary_tables(places, width):
    half = width // 2
    freqs = ROPE_BASE ** (-(jnp.arange(half, dtype=jnp.float32) * 2.0) / width)
    angles = places.astype(jnp.float32)[:, None] * freqs[None, :]
    return (jnp.cos(angles), jnp.sin(angles))


def rotate(inputs, cosine, sine):
    half = inputs.shape[-1] // 2
    first = inputs[:, :half]
    second = inputs[:, half:]
    return jnp.concatenate(
        [first * cosine - second * sine, second * cosine + first * sine], axis=-1
    )


def gelu_parts(inputs):
    inner = GELU_SCALE * (inputs + 0.044715 * inputs * inputs * inputs)
    tangent = jnp.tanh(inner)
    result = 0.5 * inputs * (1.0 + tangent)
    slope = 0.5 * (1.0 + tangent) + 0.5 * inputs * (1.0 - tangent * tangent) * GELU_SCALE * (
        1.0 + 3.0 * 0.044715 * inputs * inputs
    )
    return (result, slope)


def window_mask(segments):
    length = segments.shape[0]
    places = jnp.arange(length, dtype=jnp.int32)
    offset = places[:, None] - places[None, :]
    same = segments[:, None] == segments[None, :]
    return same & (offset >= 0) & (offset < WINDOW)


def contract_rows(left, right):
    return lax.dot_general(
        left, right, (((0,), (0,)), ((), ())), preferred_element_type=jnp.float32
    )


def contract_cols(left, right):
    return lax.dot_general(
        left, right, (((1,), (1,)), ((), ())), preferred_element_type=jnp.float32
    )


def attend_scores(queries, keys, allowed, scale):
    return jnp.where(allowed, contract_cols(queries, keys) * scale, MASKED)


def attend_forward(queries, keys, values, allowed, scale):
    scores = attend_scores(queries, keys, allowed, scale)
    top = jnp.max(scores, axis=-1, keepdims=True)
    totals = jnp.sum(jnp.exp(scores - top), axis=-1, keepdims=True)
    logsum = top + jnp.log(totals)
    probs = jnp.exp(scores - logsum).astype(jnp.bfloat16)
    return (jnp.dot(probs, values, preferred_element_type=jnp.float32), logsum)


def attend_backward(queries, keys, values, allowed, scale, logsum, grad_heads):
    probs = jnp.exp(attend_scores(queries, keys, allowed, scale) - logsum)
    grad_values = contract_rows(probs.astype(jnp.bfloat16), grad_heads)
    grad_probs = contract_cols(grad_heads, values)
    centre = jnp.sum(probs * grad_probs, axis=-1, keepdims=True)
    grad_scores = (probs * (grad_probs - centre) * scale).astype(jnp.bfloat16)
    grad_queries = jnp.dot(grad_scores, keys, preferred_element_type=jnp.float32)
    grad_keys = contract_rows(grad_scores, queries)
    return (grad_queries, grad_keys, grad_values)


def wrap(value):
    return lax.rem(value + 8, 4)


class Place:
    def __init__(self):
        dp = lax.axis_index("dp")
        self.z = lax.axis_index("tensor")
        self.core = lax.rem(dp, 2)
        self.x = lax.rem(dp // 2, 4)
        self.y = dp // 8
        self.s = 1 - 2 * self.core

    def device(self, y=None, x=None, core=None, z=None):
        y = self.y if y is None else y
        x = self.x if x is None else x
        core = self.core if core is None else core
        z = self.z if z is None else z
        return ((y * 4 + x) * 2 + core, z)

    def partner(self):
        return self.device(core=1 - self.core)

    def greet(self, xy, far_z=False):
        barrier = pltpu.get_barrier_semaphore()
        others = [self.device(z=wrap(self.z + 1)), self.device(z=wrap(self.z - 1))]
        if xy:
            others += [
                self.partner(),
                self.device(x=wrap(self.x + 1)),
                self.device(x=wrap(self.x - 1)),
                self.device(y=wrap(self.y + 1)),
                self.device(y=wrap(self.y - 1)),
            ]
        if far_z:
            others.append(self.device(z=wrap(self.z + 2)))
        for other in others:
            pl.semaphore_signal(barrier, inc=1, device_id=other, device_id_type=MESH)
        pl.semaphore_wait(barrier, len(others))


def remote(src, dst, send, recv, device):
    return pltpu.make_async_remote_copy(
        src_ref=src,
        dst_ref=dst,
        send_sem=send,
        recv_sem=recv,
        device_id=device,
        device_id_type=MESH,
    )


def merge(streams):
    waiting = []

    def advance(stream, k):
        try:
            waiting.append((next(stream), k, stream))
        except StopIteration:
            pass

    for k, stream in enumerate(streams):
        advance(stream, k)
    while waiting:
        waiting.sort(key=lambda entry: entry[:2])
        yield waiting[0][0]
        _, k, stream = waiting.pop(0)
        advance(stream, k)


def run_streams(streams):
    for _ in merge(streams):
        pass


def halves(n):
    tiles = n // 256
    a = (tiles + 1) // 2
    return (a * 128, (tiles - a) * 128)


class Axes:
    def __init__(self, place, which, n):
        wa, wb = halves(n)
        self.which = which
        self.w = wa if which == 0 else wb
        start = 0 if which == 0 else wa
        self.place = place
        self.mine = pl.ds(pl.multiple_of(place.core * (n // 2) + start, 128), self.w)
        self.theirs = pl.ds(pl.multiple_of((1 - place.core) * (n // 2) + start, 128), self.w)
        self.u, self.v = (place.x, place.y) if which == 0 else (place.y, place.x)

    def device(self, u=None, v=None):
        u = self.u if u is None else u
        v = self.v if v is None else v
        return self.place.device(y=v, x=u) if self.which == 0 else self.place.device(y=u, x=v)

    def chunk(self, ref, u, v, cols):
        return ref.at[v, u, :, cols] if self.which == 0 else ref.at[u, v, :, cols]

    def group(self, ref, v, cols):
        return ref.at[v, :, :, cols] if self.which == 0 else ref.at[:, v, :, cols]


def merge_own(place, own, other, both, send, recv):
    copy = remote(own, other, send, recv, place.partner())
    copy.start()
    yield 2
    copy.wait()
    mine = own[...].astype(F32)
    theirs = other[...].astype(F32)
    first = place.core == 0
    both[...] = jnp.concatenate(
        [jnp.where(first, mine, theirs), jnp.where(first, theirs, mine)], axis=0
    ).astype(BF16)


def gather_half(ax, both, out, base, ring_send, ring_recv, chip_send, chip_recv):
    place, s = ax.place, ax.place.s
    cols = ax.mine
    sent = []

    def send(src, u, v, device, k):
        copy = remote(src, ax.chunk(out, u, v, cols), ring_send.at[k], ring_recv.at[k], device)
        copy.start()
        sent.append(copy)

    def arrive(u, v, k):
        here = ax.chunk(out, u, v, cols)
        remote(here, here, ring_send.at[k], ring_recv.at[k], place.partner()).wait_recv()
        copy = remote(here, here, chip_send.at[k], chip_recv.at[k], place.partner())
        copy.start()
        sent.append(copy)

    def along_v(src, u, r):
        send(src, u, ax.v, ax.device(v=wrap(ax.v + s)), 3 + 3 * r)
        send(src, u, ax.v, ax.device(v=wrap(ax.v - s)), 4 + 3 * r)

    own = both.at[:, cols]
    us = [ax.u, wrap(ax.u - s), wrap(ax.u + s), wrap(ax.u + 2)]
    send(own, ax.u, ax.v, ax.device(u=wrap(ax.u + s)), 0)
    send(own, ax.u, ax.v, ax.device(u=wrap(ax.u - s)), 1)
    along_v(own, ax.u, 0)
    yield base + 3
    arrive(us[1], ax.v, 0)
    src = ax.chunk(out, us[1], ax.v, cols)
    send(src, us[1], ax.v, ax.device(u=wrap(ax.u + s)), 2)
    along_v(src, us[1], 1)
    yield base + 3
    arrive(us[2], ax.v, 1)
    along_v(ax.chunk(out, us[2], ax.v, cols), us[2], 2)
    yield base + 5
    for r in range(4):
        if r == 1:
            arrive(us[3], ax.v, 2)
            along_v(ax.chunk(out, us[3], ax.v, cols), us[3], 3)
            yield base + 6
        v = wrap(ax.v - s)
        arrive(us[r], v, 3 + 3 * r)
        send(ax.chunk(out, us[r], v, cols), us[r], v, ax.device(v=wrap(ax.v + s)), 5 + 3 * r)
        yield base + 4.5 + 2.5 * r
        arrive(us[r], wrap(ax.v + s), 4 + 3 * r)
        yield base + (5 if r == 0 else 4 + 2.5 * (r + 1))
    for r in range(4):
        arrive(us[r], wrap(ax.v + 2), 5 + 3 * r)
        yield base + 14 + r
    yield 90
    for copy in sent:
        copy.wait_send()
    theirs = [ax.u, wrap(ax.u + s), wrap(ax.u - s), wrap(ax.u + 2)]
    landing = [(theirs[1], ax.v), (theirs[2], ax.v), (theirs[3], ax.v)]
    for r in range(4):
        landing += [(theirs[r], wrap(ax.v + s)), (theirs[r], wrap(ax.v - s)), (theirs[r], wrap(ax.v + 2))]
    for k, (u, v) in enumerate(landing):
        here = ax.chunk(out, u, v, ax.theirs)
        remote(here, here, chip_send.at[k], chip_recv.at[k], place.partner()).wait_recv()


def gather_stream(place, own, out, scratch, base=0):
    other, both, sems, local = scratch
    n = own.shape[1]
    yield from merge_own(place, own, other, both, sems.at[0, 0, 0, 15], sems.at[0, 0, 1, 15])
    keep = pltpu.make_async_copy(both, out.at[place.y, place.x], local)
    keep.start()
    yield base + 2
    yield from merge(
        [
            gather_half(
                Axes(place, h, n), both, out, base + 2,
                sems.at[h, 0, 0], sems.at[h, 0, 1], sems.at[h, 1, 0], sems.at[h, 1, 1],
            )
            for h in (0, 1)
        ]
    )
    keep.wait()


def gather_scratch(n):
    return [
        pltpu.VMEM((36, n), BF16),
        pltpu.VMEM((CHUNK, n), BF16),
        pltpu.SemaphoreType.DMA((2, 2, 2, 16)),
        pltpu.SemaphoreType.DMA,
    ]


def add_chunks(count, target, *terms):
    def body(i, carry):
        total = terms[0](i)[...].astype(F32)
        for term in terms[1:]:
            total = total + term(i)[...].astype(F32)
        target(i)[...] = total.astype(BF16)
        return carry

    if count == 1:
        body(0, 0)
    else:
        lax.fori_loop(0, count, body, 0)


def scatter_half(ax, grads, final, bufs, sems, base):
    held, got, b1, b2, b3, c1, c2, c3, total = bufs
    place, s = ax.place, ax.place.s
    vs = [wrap(ax.v + 2), wrap(ax.v - s), wrap(ax.v + s), ax.v]
    for_partner = [wrap(ax.v + 2), wrap(ax.v + s), wrap(ax.v - s), ax.v]
    sent, loads, gets = [], [], []
    yield base
    for k in range(4):
        give = remote(
            ax.group(grads, for_partner[k], ax.theirs),
            got.at[k],
            sems.at[0, k],
            sems.at[1, k],
            place.partner(),
        )
        give.start()
        sent.append(give)
        gets.append(give)
        load = pltpu.make_async_copy(ax.group(grads, vs[k], ax.mine), held.at[k], sems.at[2, k])
        load.start()
        loads.append(load)
    yield base + 3

    def chip_sum(k):
        loads[k].wait()
        gets[k].wait_recv()
        add_chunks(4, lambda i: got.at[k, i], lambda i: got.at[k, i], lambda i: held.at[k, i])

    def send(src, dst, k, device):
        copy = remote(src, dst, sems.at[0, k], sems.at[1, k], device)
        copy.start()
        sent.append(copy)
        return copy

    chip_sum(0)
    far = send(got.at[0], b1, 4, ax.device(v=wrap(ax.v + s)))
    yield base + 4
    chip_sum(1)
    back = send(got.at[1], b2, 5, ax.device(v=wrap(ax.v - s)))
    yield base + 6
    chip_sum(2)
    yield base + 8
    far.wait_recv()
    add_chunks(4, lambda i: b1.at[i], lambda i: b1.at[i], lambda i: got.at[2, i])
    forth = send(b1, b3, 6, ax.device(v=wrap(ax.v + s)))
    yield base + 9
    loads[3].wait()
    gets[3].wait_recv()
    back.wait_recv()
    yield base + 13
    forth.wait_recv()
    add_chunks(
        4,
        lambda i: total.at[i],
        lambda i: got.at[3, i],
        lambda i: held.at[3, i],
        lambda i: b2.at[i],
        lambda i: b3.at[i],
    )
    far = send(total.at[wrap(ax.u + 2)], c1, 7, ax.device(u=wrap(ax.u + s)))
    back = send(total.at[wrap(ax.u - s)], c2, 8, ax.device(u=wrap(ax.u - s)))
    yield base + 17
    far.wait_recv()
    add_chunks(1, lambda i: c1, lambda i: c1, lambda i: total.at[wrap(ax.u + s)])
    forth = send(c1, c3, 9, ax.device(u=wrap(ax.u + s)))
    yield base + 21
    back.wait_recv()
    forth.wait_recv()
    add_chunks(1, lambda i: c2, lambda i: total.at[ax.u], lambda i: c2, lambda i: c3)
    keep = pltpu.make_async_copy(c2, final.at[:, ax.mine], sems.at[2, 4])
    keep.start()
    last = send(c2, final.at[:, ax.mine], 10, place.partner())
    yield 90
    for copy in sent:
        copy.wait_send()
    keep.wait()
    remote(c2, final.at[:, ax.theirs], sems.at[0, 10], sems.at[1, 10], place.partner()).wait_recv()


def scatter_scratch(n):
    shapes = []
    for w in halves(n):
        shapes += [pltpu.VMEM((4, 4, CHUNK, w), BF16)] * 2
        shapes += [pltpu.VMEM((4, CHUNK, w), BF16)] * 3
        shapes += [pltpu.VMEM((CHUNK, w), BF16)] * 3
        shapes += [pltpu.VMEM((4, CHUNK, w), BF16)]
        shapes += [pltpu.SemaphoreType.DMA((3, 11))]
    return shapes


def scatter_streams(place, grads, final, scratch, base=0):
    n = grads.shape[3]
    for h in (0, 1):
        part = scratch[10 * h : 10 * h + 10]
        yield scatter_half(Axes(place, h, n), grads, final, part[:9], part[9], base)


def rows_gather(place, out, sems, base=0):
    s, z = place.s, place.z
    ahead, behind = place.device(z=wrap(z + s)), place.device(z=wrap(z - s))

    def copy(slot, k, device):
        return remote(out.at[slot], out.at[slot], sems.at[0, k], sems.at[1, k], device)

    first = copy(z, 0, ahead)
    first.start()
    second = copy(z, 1, behind)
    second.start()
    yield base + 9
    copy(wrap(z - s), 0, ahead).wait_recv()
    relay = copy(wrap(z - s), 2, ahead)
    relay.start()
    yield base + 9.5
    copy(wrap(z + s), 1, ahead).wait_recv()
    yield base + 14
    copy(wrap(z + 2), 2, ahead).wait_recv()
    for sent in (first, second, relay):
        sent.wait_send()


def rows_scatter(place, parts, bufs, sems):
    s, z = place.s, place.z
    b1, b2, b3 = bufs
    ahead, behind = place.device(z=wrap(z + s)), place.device(z=wrap(z - s))

    def copy(src, dst, k, device):
        return remote(src, dst, sems.at[0, k], sems.at[1, k], device)

    far = copy(parts.at[wrap(z + 2)], b1, 0, ahead)
    far.start()
    back = copy(parts.at[wrap(z - s)], b2, 1, behind)
    back.start()
    yield 9
    far.wait_recv()
    mid = wrap(z + s)

    def body(i, carry):
        rows = pl.ds(pl.multiple_of(i * 32, 32), 32)
        b1[rows, :] = (b1[rows, :].astype(F32) + parts[mid, rows, :].astype(F32)).astype(BF16)
        return carry

    lax.fori_loop(0, ROWS // 32, body, 0)
    forth = copy(b1, b3, 2, ahead)
    forth.start()
    yield 10
    back.wait_recv()
    yield 15
    forth.wait_recv()
    for sent in (far, back, forth):
        sent.wait_send()


def rows_scratch():
    return [pltpu.VMEM((ROWS, WIDTH), BF16)] * 3 + [pltpu.SemaphoreType.DMA((2, 3))] * 2


def row_blocks(body):
    def step(i, carry):
        body(pl.ds(pl.multiple_of(i * 16, 16), 16))
        return carry

    lax.fori_loop(0, ROWS // 16, step, 0)


def col_sum(ref, row, values):
    ref[8 * row : 8 * row + 8, :] = ref[8 * row : 8 * row + 8, :] + values[:8] + values[8:]


def start_kernel(tokens, attn_own, own_g, rows_out, mats_out, full_g, sems, *scratch):
    place = Place()
    place.greet(True)

    def z_stream():
        rows_out[place.z] = tokens[...]
        yield from rows_gather(place, rows_out, sems)

    run_streams(
        [
            gather_stream(place, attn_own, mats_out, scratch[:4]),
            gather_stream(place, own_g, full_g, scratch[4:8], 6),
            z_stream(),
        ]
    )


def middle_kernel(parts, tokens, gains, own_u, own_d, rows_out, attn_sum, full_u, full_d, *scratch):
    place = Place()
    place.greet(True)
    b1, b2, b3, sems, sems2 = scratch[:5]

    def z_stream():
        yield from rows_scatter(place, parts, (b1, b2, b3), sems)

        def body(rows):
            total = (
                parts[place.z, rows, :].astype(F32) + b2[rows, :].astype(F32) + b3[rows, :].astype(F32)
            )
            attn_sum[rows, :] = total
            hat, _ = normalize(total)
            hidden = tokens[rows, :].astype(F32) + hat * gains[1:2, :]
            mid, _ = normalize(hidden)
            rows_out[place.z, rows, :] = (mid * gains[2:3, :]).astype(BF16)

        row_blocks(body)
        yield from rows_gather(place, rows_out, sems2, 17)

    run_streams(
        [
            z_stream(),
            gather_stream(place, own_u, full_u, scratch[5:9]),
            gather_stream(place, own_d, full_d, scratch[9:13], 9),
        ]
    )


def turn_kernel(
    parts, tokens, attn_sum, gains, cotangent, gate, upward, rows_out, layer_out, sums, by_gate, by_up, *scratch
):
    place = Place()
    place.greet(False)
    b1, b2, b3, sems, sems2 = scratch[:5]
    sums[...] = jnp.zeros_like(sums)

    def z_stream():
        yield from rows_scatter(place, parts, (b1, b2, b3), sems)

        def body(rows):
            total = (
                parts[place.z, rows, :].astype(F32) + b2[rows, :].astype(F32) + b3[rows, :].astype(F32)
            )
            attn_hat, _ = normalize(attn_sum[rows, :])
            hidden = tokens[rows, :].astype(F32) + attn_hat * gains[1:2, :]
            hat, inverse = normalize(total)
            layer_out[rows, :] = (hidden + hat * gains[3:4, :]).astype(BF16)
            grad = cotangent[rows, :].astype(F32)
            col_sum(sums, 0, grad * hat)
            rows_out[place.z, rows, :] = normalize_back(grad * gains[3:4, :], hat, inverse).astype(BF16)

        row_blocks(body)
        yield from rows_gather(place, rows_out, sems2, 17)

    held_g, held_u, moves = scratch[5:8]

    def gelu_stream():
        def load(i):
            return (
                pltpu.make_async_copy(gate.at[i], held_g.at[i], moves.at[0, i]),
                pltpu.make_async_copy(upward.at[i], held_u.at[i], moves.at[1, i]),
            )

        def store(i):
            return (
                pltpu.make_async_copy(held_g.at[i], by_gate.at[i], moves.at[0, i]),
                pltpu.make_async_copy(held_u.at[i], by_up.at[i], moves.at[1, i]),
            )

        for i in range(8):
            for copy in load(i):
                copy.start()
        for i in range(8):
            yield (1 + i if i < 4 else 7 + i)
            for copy in load(i):
                copy.wait()

            def step(k, carry):
                rows = pl.ds(pl.multiple_of(k * 8, 8), 8)
                value, slope = gelu_parts(held_g[i, rows, :])
                held_g[i, rows, :] = held_u[i, rows, :] * slope
                held_u[i, rows, :] = value
                return carry

            lax.fori_loop(0, 10, step, 0)
            for copy in store(i):
                copy.start()
        yield 80
        for i in range(8):
            for copy in store(i):
                copy.wait()

    run_streams([z_stream(), gelu_stream()])


def back_kernel(
    parts, tokens, attn_sum, gains, cotangent, grad_d, grad_g,
    rows_out, grad_hidden, sums, sum_d, sum_g, *scratch
):
    place = Place()
    place.greet(True)
    b1, b2, b3, sems, sems2 = scratch[:5]
    sums[...] = jnp.zeros_like(sums)

    def z_stream():
        yield from rows_scatter(place, parts, (b1, b2, b3), sems)

        def body(rows):
            grad_mid = (
                parts[place.z, rows, :].astype(F32) + b2[rows, :].astype(F32) + b3[rows, :].astype(F32)
            )
            attn_hat, attn_inverse = normalize(attn_sum[rows, :])
            hidden = tokens[rows, :].astype(F32) + attn_hat * gains[1:2, :]
            mid, inverse = normalize(hidden)
            col_sum(sums, 0, grad_mid * mid)
            grad = cotangent[rows, :].astype(F32) + normalize_back(grad_mid * gains[2:3, :], mid, inverse)
            grad_hidden[rows, :] = grad
            col_sum(sums, 1, grad * attn_hat)
            rows_out[place.z, rows, :] = normalize_back(
                grad * gains[1:2, :], attn_hat, attn_inverse
            ).astype(BF16)

        row_blocks(body)
        yield from rows_gather(place, rows_out, sems2, 17)

    streams = [z_stream()]
    for i, (grads, final) in enumerate(((grad_d, sum_d), (grad_g, sum_g))):
        streams += list(scatter_streams(place, grads, final, scratch[5 + 20 * i : 25 + 20 * i], 9 * i))
    run_streams(streams)


def end_kernel(parts, grads, grad_u, grad_rows, final, shared, sum_u, *scratch):
    place = Place()
    place.greet(True, far_z=True)
    b1, b2, b3, sems, sems2 = scratch[:5]
    got, zsend, zrecv = scratch[5:8]

    def z_stream():
        yield from rows_scatter(place, parts, (b1, b2, b3), sems)

        def body(rows):
            grad_rows[rows, :] = (
                parts[place.z, rows, :].astype(F32) + b2[rows, :].astype(F32) + b3[rows, :].astype(F32)
            )

        row_blocks(body)

    def attn_stream():
        yield from merge(scatter_streams(place, grads, final, scratch[8:28]))
        cols = pl.ds(512, 768)
        copies = []
        for k in range(3):
            copy = remote(
                final.at[:, cols], got.at[k], zsend.at[k], zrecv.at[k], place.device(z=wrap(place.z + k + 1))
            )
            copy.start()
            copies.append(copy)
        yield 95
        for copy in copies:
            copy.wait()
        total = final[:, cols].astype(F32)
        for k in range(3):
            total = total + got[k].astype(F32)
        shared[...] = total

    run_streams([attn_stream(), z_stream()] + list(scatter_streams(place, grad_u, sum_u, scratch[28:48], 5)))


def call(kernel, outs, ins, spaces, out_spaces, scratch, ident):
    return pl.pallas_call(
        kernel,
        out_shape=[jax.ShapeDtypeStruct(shape, dtype) for shape, dtype in outs],
        in_specs=[pl.BlockSpec(memory_space=space) for space in spaces],
        out_specs=[pl.BlockSpec(memory_space=space) for space in out_spaces],
        scratch_shapes=scratch,
        compiler_params=pltpu.CompilerParams(
            collective_id=ident, has_side_effects=True, vmem_limit_bytes=60 * 1024 * 1024
        ),
        name=kernel.__name__,
    )(*ins)


def local(
    tokens,
    cotangent,
    segment_ids,
    positions,
    w_query,
    w_key,
    w_value,
    w_out,
    w_gate,
    w_up,
    w_down,
    prenorm_attn,
    postnorm_attn,
    prenorm_ffw,
    postnorm_ffw,
    query_norm,
    key_norm,
):
    vm, hbm = pltpu.VMEM, pl.ANY
    shard = 36
    core = lax.rem(lax.axis_index("dp"), 2)
    hidden_units = w_gate.shape[1]
    pad = ((0, 0), (0, FFPAD - hidden_units))
    width = w_key.shape[1]

    def column(vector):
        return jnp.pad(vector, (0, shard - vector.shape[0]))[:, None]

    attn_own = jnp.concatenate(
        [w_query, w_out.T, w_key, w_value]
        + [column(g) for g in (prenorm_attn, postnorm_attn, prenorm_ffw, postnorm_ffw, query_norm, key_norm)]
        + [jnp.zeros((shard, ATTN_COLS - 1024 - 6), BF16)],
        axis=1,
    )
    whole = ((4, 4, CHUNK, FFPAD), BF16)
    tokens_all, mats, full_gate = call(
        start_kernel,
        [((4, ROWS, WIDTH), BF16), ((4, 4, CHUNK, ATTN_COLS), BF16), whole],
        [tokens, attn_own, jnp.pad(w_gate, pad)],
        [vm, vm, vm],
        [vm, hbm, hbm],
        [pltpu.SemaphoreType.DMA((2, 3))] + gather_scratch(ATTN_COLS) + gather_scratch(FFPAD),
        0,
    )
    mats = mats.reshape(WIDTH, ATTN_COLS)
    full_query, full_out = mats[:, :256], mats[:, 256:512]
    full_key, full_value = mats[:, 512:768], mats[:, 768:1024]
    small = mats[:, 1024:1032].astype(F32).T
    gains = small
    gain_in = small[0]
    gain_query = small[4].reshape(32, shard)[:, :8].reshape(-1)
    gain_key = small[5].reshape(32, shard)[:, :8].reshape(-1)
    normed_all, _ = normalize(tokens_all.reshape(4 * ROWS, WIDTH).astype(F32))
    attn_rows = (normed_all * gain_in).astype(BF16)
    scale = 1.0 / math.sqrt(width)
    cosine, sine = rotary_tables(positions.reshape(-1), width)
    mask = window_mask(segment_ids[0])
    key_hat, key_inverse = normalize(jnp.dot(attn_rows, full_key, preferred_element_type=F32))
    keys = rotate(key_hat * gain_key, cosine, sine).astype(BF16)
    values = jnp.dot(attn_rows, full_value, preferred_element_type=F32).astype(BF16)
    query_hat, query_inverse = normalize(jnp.dot(attn_rows, full_query, preferred_element_type=F32))
    queries = rotate(query_hat * gain_query, cosine, sine).astype(BF16)
    piece, logsum = attend_forward(queries, keys, values, mask, scale)
    heads_out = piece.astype(BF16)
    attn_part = contract_cols(heads_out, full_out).astype(BF16)
    ffw_rows, attn_sum, full_up, full_down = call(
        middle_kernel,
        [((4, ROWS, WIDTH), BF16), ((ROWS, WIDTH), F32), whole, whole],
        [
            attn_part.reshape(4, ROWS, WIDTH),
            tokens,
            gains,
            jnp.pad(w_up, pad),
            jnp.pad(w_down.T, pad),
        ],
        [vm] * 5,
        [vm, vm, hbm, hbm],
        rows_scratch() + gather_scratch(FFPAD) * 2,
        1,
    )
    ffw_rows = ffw_rows.reshape(4 * ROWS, WIDTH)
    full_gate = full_gate.reshape(WIDTH, FFPAD)
    full_up = full_up.reshape(WIDTH, FFPAD)
    full_down = full_down.reshape(WIDTH, FFPAD)
    gate = jnp.dot(ffw_rows, full_gate, preferred_element_type=F32)
    upward = jnp.dot(ffw_rows, full_up, preferred_element_type=F32)
    gelu_value, _ = gelu_parts(gate)
    act = (gelu_value * upward).astype(BF16)
    ffw_part = contract_cols(act, full_down).astype(BF16)
    blocks = (8, 80, FFPAD)
    grad_ffw, layer_out, ffw_sums, by_gate, by_up = call(
        turn_kernel,
        [((4, ROWS, WIDTH), BF16), ((ROWS, WIDTH), BF16), ((8, WIDTH), F32), (blocks, F32), (blocks, F32)],
        [
            ffw_part.reshape(4, ROWS, WIDTH),
            tokens,
            attn_sum,
            gains,
            cotangent,
            gate.reshape(blocks),
            upward.reshape(blocks),
        ],
        [vm] * 5 + [hbm] * 2,
        [vm] * 3 + [hbm] * 2,
        rows_scratch() + [pltpu.VMEM(blocks, F32)] * 2 + [pltpu.SemaphoreType.DMA((2, 8))],
        2,
    )
    grad_ffw = grad_ffw.reshape(4 * ROWS, WIDTH)
    grad_down = contract_rows(grad_ffw, act).astype(BF16)
    grad_act = jnp.dot(grad_ffw, full_down, preferred_element_type=F32)
    grad_gate_in = (grad_act * by_gate.reshape(4 * ROWS, FFPAD)).astype(BF16)
    grad_up_in = (grad_act * by_up.reshape(4 * ROWS, FFPAD)).astype(BF16)
    grad_gate = contract_rows(ffw_rows, grad_gate_in).astype(BF16)
    grad_up = contract_rows(ffw_rows, grad_up_in).astype(BF16)
    mid_part = (contract_cols(grad_gate_in, full_gate) + contract_cols(grad_up_in, full_up)).astype(BF16)
    split = (4, 4, CHUNK, FFPAD)
    final = ((CHUNK, FFPAD), BF16)
    grad_attn, grad_hidden, mid_sums, sum_down, sum_gate = call(
        back_kernel,
        [((4, ROWS, WIDTH), BF16), ((ROWS, WIDTH), F32), ((16, WIDTH), F32), final, final],
        [
            mid_part.reshape(4, ROWS, WIDTH),
            tokens,
            attn_sum,
            gains,
            cotangent,
            grad_down.reshape(split),
            grad_gate.reshape(split),
        ],
        [vm] * 5 + [hbm] * 2,
        [vm] * 5,
        rows_scratch() + scatter_scratch(FFPAD) * 2,
        3,
    )
    grad_attn = grad_attn.reshape(4 * ROWS, WIDTH)
    grad_output = contract_rows(grad_attn, heads_out)
    grad_heads = jnp.dot(grad_attn, full_out, preferred_element_type=F32).astype(BF16)
    grad_queries, grad_keys, grad_values = attend_backward(
        queries, keys, values, mask, scale, logsum, grad_heads
    )
    grad_query_turned = rotate(grad_queries, cosine, -sine)
    grad_query_norm = jnp.sum(grad_query_turned * query_hat, axis=0)
    query_in = normalize_back(grad_query_turned * gain_query, query_hat, query_inverse).astype(BF16)
    grad_key_turned = rotate(grad_keys, cosine, -sine)
    grad_key_norm = jnp.sum(grad_key_turned * key_hat, axis=0)
    key_in = normalize_back(grad_key_turned * gain_key, key_hat, key_inverse).astype(BF16)
    value_in = grad_values.astype(BF16)
    grad_query = contract_rows(attn_rows, query_in)
    grad_key = contract_rows(attn_rows, key_in)
    grad_value = contract_rows(attn_rows, value_in)
    in_part = contract_cols(query_in, full_query)
    in_part = in_part + contract_cols(key_in, full_key)
    in_part = in_part + contract_cols(value_in, full_value)
    grad_pre_attn = jnp.sum(in_part * normed_all, axis=0)

    def placed_rows(vector):
        return jnp.pad(vector.reshape(32, 8), ((0, 0), (0, shard - 8))).reshape(-1)

    vectors = jnp.stack(
        [
            grad_pre_attn,
            jnp.sum(mid_sums[8:], axis=0),
            jnp.sum(mid_sums[:8], axis=0),
            jnp.sum(ffw_sums, axis=0),
            placed_rows(grad_query_norm),
            placed_rows(grad_key_norm),
        ]
    )
    small_grads = jnp.pad(vectors, ((0, ATTN_COLS - 1024 - 6), (0, 0))).T
    grads = jnp.concatenate(
        [g.astype(BF16) for g in (grad_query, grad_output, grad_key, grad_value, small_grads)], axis=1
    )
    grad_in_rows, sum_attn, sum_shared, sum_up = call(
        end_kernel,
        [((ROWS, WIDTH), F32), ((CHUNK, ATTN_COLS), BF16), ((CHUNK, ATTN_COLS - 512), F32), final],
        [
            in_part.astype(BF16).reshape(4, ROWS, WIDTH),
            grads.reshape(4, 4, CHUNK, ATTN_COLS),
            grad_up.reshape(split),
        ],
        [vm, hbm, hbm],
        [vm] * 4,
        rows_scratch()
        + [
            pltpu.VMEM((3, CHUNK, ATTN_COLS - 512), BF16),
            pltpu.SemaphoreType.DMA((3,)),
            pltpu.SemaphoreType.DMA((3,)),
        ]
        + scatter_scratch(ATTN_COLS)
        + scatter_scratch(FFPAD),
        4,
    )
    normed_in, inverse_in = normalize(tokens.astype(F32))
    grad_tokens = grad_hidden + normalize_back(grad_in_rows * gain_in, normed_in, inverse_in)

    def own_rows(array):
        first = core == 0
        return jnp.where(first, array[:shard], array[shard:]).astype(F32)

    own_attn = own_rows(sum_attn[:, :512])
    own_shared = own_rows(sum_shared)
    own_small = own_shared[:, 512:520]
    return (
        layer_out,
        grad_tokens,
        own_attn[:, :256],
        own_shared[:, :256],
        own_shared[:, 256:512],
        own_attn[:, 256:].T,
        own_rows(sum_gate)[:, :hidden_units],
        own_rows(sum_up)[:, :hidden_units],
        own_rows(sum_down)[:, :hidden_units].T,
        own_small[:, 0],
        own_small[:, 1],
        own_small[:, 2],
        own_small[:, 3],
        own_small[:8, 4],
        own_small[:8, 5],
    )


def solution(mesh):
    placed = (
        P(("dp", "tensor"), None),
        P(("dp", "tensor"), None),
        P("dp", None),
        P("dp", None),
        P("dp", "tensor"),
        P("dp", None),
        P("dp", None),
        P("tensor", "dp"),
        P("dp", "tensor"),
        P("dp", "tensor"),
        P("tensor", "dp"),
        P("dp"),
        P("dp"),
        P("dp"),
        P("dp"),
        P("dp"),
        P("dp"),
    )
    return jax.shard_map(
        local,
        mesh=mesh,
        in_specs=placed,
        out_specs=(
            P(("dp", "tensor"), None),
            P(("dp", "tensor"), None),
            P("dp", "tensor"),
            P("dp", None),
            P("dp", None),
            P("tensor", "dp"),
            P("dp", "tensor"),
            P("dp", "tensor"),
            P("tensor", "dp"),
            P("dp"),
            P("dp"),
            P("dp"),
            P("dp"),
            P("dp"),
            P("dp"),
        ),
        check_vma=False,
    )
```

```python
import functools
import math

import jax
import jax.numpy as jnp
from jax import lax
from jax.experimental import pallas as pl
from jax.experimental.pallas import tpu as pltpu
from jax.sharding import PartitionSpec as P

WINDOW = 512
EPSILON = 1e-06
ROPE_BASE = 10000.0
GELU_SCALE = math.sqrt(2.0 / math.pi)
MASKED = -1e30
BF16 = jnp.bfloat16
F32 = jnp.float32
ROWS = 160
WIDTH = 1152
CHUNK = 72
FFPAD = 1792
ATTN_COLS = 1280
MESH = pl.DeviceIdType.MESH

GATHER_AT = (4.5, 7.5, 7.0, 5.0, 5.0)
SCATTER_AT = (4, 6, 8, 9, 13, 13.5, 20, 24, 27)
ROWS_AT = (6, 10, 10.5, 12, 15)


def normalize(inputs):
    inverse = lax.rsqrt(jnp.mean(inputs * inputs, axis=-1, keepdims=True) + EPSILON)
    return (inputs * inverse, inverse)


def normalize_back(grad_hat, normed, inverse):
    return inverse * (grad_hat - normed * jnp.mean(grad_hat * normed, axis=-1, keepdims=True))


def rotary_tables(places, width):
    half = width // 2
    freqs = ROPE_BASE ** (-(jnp.arange(half, dtype=jnp.float32) * 2.0) / width)
    angles = places.astype(jnp.float32)[:, None] * freqs[None, :]
    return (jnp.cos(angles), jnp.sin(angles))


def rotate(inputs, cosine, sine):
    half = inputs.shape[-1] // 2
    first = inputs[:, :half]
    second = inputs[:, half:]
    return jnp.concatenate(
        [first * cosine - second * sine, second * cosine + first * sine], axis=-1
    )


def gelu_parts(inputs):
    inner = GELU_SCALE * (inputs + 0.044715 * inputs * inputs * inputs)
    tangent = jnp.tanh(inner)
    result = 0.5 * inputs * (1.0 + tangent)
    slope = 0.5 * (1.0 + tangent) + 0.5 * inputs * (1.0 - tangent * tangent) * GELU_SCALE * (
        1.0 + 3.0 * 0.044715 * inputs * inputs
    )
    return (result, slope)


def window_mask(segments):
    length = segments.shape[0]
    places = jnp.arange(length, dtype=jnp.int32)
    offset = places[:, None] - places[None, :]
    same = segments[:, None] == segments[None, :]
    return same & (offset >= 0) & (offset < WINDOW)


def contract_rows(left, right):
    return lax.dot_general(
        left, right, (((0,), (0,)), ((), ())), preferred_element_type=jnp.float32
    )


def contract_cols(left, right):
    return lax.dot_general(
        left, right, (((1,), (1,)), ((), ())), preferred_element_type=jnp.float32
    )


def attend_scores(queries, keys, allowed, scale):
    return jnp.where(allowed, contract_cols(queries, keys) * scale, MASKED)


def attend_forward(queries, keys, values, allowed, scale):
    scores = attend_scores(queries, keys, allowed, scale)
    top = jnp.max(scores, axis=-1, keepdims=True)
    totals = jnp.sum(jnp.exp(scores - top), axis=-1, keepdims=True)
    logsum = top + jnp.log(totals)
    probs = jnp.exp(scores - logsum).astype(jnp.bfloat16)
    return (jnp.dot(probs, values, preferred_element_type=jnp.float32), logsum)


def attend_backward(queries, keys, values, allowed, scale, logsum, grad_heads):
    probs = jnp.exp(attend_scores(queries, keys, allowed, scale) - logsum)
    grad_values = contract_rows(probs.astype(jnp.bfloat16), grad_heads)
    grad_probs = contract_cols(grad_heads, values)
    centre = jnp.sum(probs * grad_probs, axis=-1, keepdims=True)
    grad_scores = (probs * (grad_probs - centre) * scale).astype(jnp.bfloat16)
    grad_queries = jnp.dot(grad_scores, keys, preferred_element_type=jnp.float32)
    grad_keys = contract_rows(grad_scores, queries)
    return (grad_queries, grad_keys, grad_values)


def wrap(value):
    return lax.rem(value + 8, 4)


class Place:
    def __init__(self):
        dp = lax.axis_index("dp")
        self.z = lax.axis_index("tensor")
        self.core = lax.rem(dp, 2)
        self.x = lax.rem(dp // 2, 4)
        self.y = dp // 8
        self.s = 1 - 2 * self.core

    def device(self, y=None, x=None, core=None, z=None):
        y = self.y if y is None else y
        x = self.x if x is None else x
        core = self.core if core is None else core
        z = self.z if z is None else z
        return ((y * 4 + x) * 2 + core, z)

    def partner(self):
        return self.device(core=1 - self.core)

    def greet(self, xy, far_z=False):
        barrier = pltpu.get_barrier_semaphore()
        others = [self.device(z=wrap(self.z + 1)), self.device(z=wrap(self.z - 1))]
        if xy:
            others += [
                self.partner(),
                self.device(x=wrap(self.x + 1)),
                self.device(x=wrap(self.x - 1)),
                self.device(y=wrap(self.y + 1)),
                self.device(y=wrap(self.y - 1)),
            ]
        if far_z:
            others.append(self.device(z=wrap(self.z + 2)))
        for other in others:
            pl.semaphore_signal(barrier, inc=1, device_id=other, device_id_type=MESH)
        pl.semaphore_wait(barrier, len(others))


def remote(src, dst, send, recv, device):
    return pltpu.make_async_remote_copy(
        src_ref=src,
        dst_ref=dst,
        send_sem=send,
        recv_sem=recv,
        device_id=device,
        device_id_type=MESH,
    )


def merge(streams):
    waiting = []

    def advance(stream, k):
        try:
            waiting.append((next(stream), k, stream))
        except StopIteration:
            pass

    for k, stream in enumerate(streams):
        advance(stream, k)
    while waiting:
        waiting.sort(key=lambda entry: entry[:2])
        yield waiting[0][0]
        _, k, stream = waiting.pop(0)
        advance(stream, k)


def run_streams(streams):
    for _ in merge(streams):
        pass


def halves(n):
    tiles = n // 256
    a = (tiles + 1) // 2
    return (a * 128, (tiles - a) * 128)


class Axes:
    def __init__(self, place, which, n):
        wa, wb = halves(n)
        self.which = which
        self.w = wa if which == 0 else wb
        start = 0 if which == 0 else wa
        self.place = place
        self.mine = pl.ds(pl.multiple_of(place.core * (n // 2) + start, 128), self.w)
        self.theirs = pl.ds(pl.multiple_of((1 - place.core) * (n // 2) + start, 128), self.w)
        self.u, self.v = (place.x, place.y) if which == 0 else (place.y, place.x)

    def device(self, u=None, v=None):
        u = self.u if u is None else u
        v = self.v if v is None else v
        return self.place.device(y=v, x=u) if self.which == 0 else self.place.device(y=u, x=v)

    def chunk(self, ref, u, v, cols):
        return ref.at[v, u, :, cols] if self.which == 0 else ref.at[u, v, :, cols]

    def group(self, ref, v, cols):
        return ref.at[v, :, :, cols] if self.which == 0 else ref.at[:, v, :, cols]


def merge_own(place, own, other, both, send, recv):
    copy = remote(own, other, send, recv, place.partner())
    copy.start()
    yield 2
    copy.wait()
    mine = own[...].astype(F32)
    theirs = other[...].astype(F32)
    first = place.core == 0
    both[...] = jnp.concatenate(
        [jnp.where(first, mine, theirs), jnp.where(first, theirs, mine)], axis=0
    ).astype(BF16)


def gather_half(ax, both, out, base, ring_send, ring_recv, chip_send, chip_recv):
    place, s = ax.place, ax.place.s
    cols = ax.mine
    sent = []

    def send(src, u, v, device, k):
        copy = remote(src, ax.chunk(out, u, v, cols), ring_send.at[k], ring_recv.at[k], device)
        copy.start()
        sent.append(copy)

    def arrive(u, v, k):
        here = ax.chunk(out, u, v, cols)
        remote(here, here, ring_send.at[k], ring_recv.at[k], place.partner()).wait_recv()
        copy = remote(here, here, chip_send.at[k], chip_recv.at[k], place.partner())
        copy.start()
        sent.append(copy)

    def along_v(src, u, r):
        send(src, u, ax.v, ax.device(v=wrap(ax.v + s)), 3 + 3 * r)
        send(src, u, ax.v, ax.device(v=wrap(ax.v - s)), 4 + 3 * r)

    own = both.at[:, cols]
    us = [ax.u, wrap(ax.u - s), wrap(ax.u + s), wrap(ax.u + 2)]
    send(own, ax.u, ax.v, ax.device(u=wrap(ax.u + s)), 0)
    send(own, ax.u, ax.v, ax.device(u=wrap(ax.u - s)), 1)
    along_v(own, ax.u, 0)
    yield base + GATHER_AT[0]
    arrive(us[1], ax.v, 0)
    src = ax.chunk(out, us[1], ax.v, cols)
    send(src, us[1], ax.v, ax.device(u=wrap(ax.u + s)), 2)
    along_v(src, us[1], 1)
    yield base + GATHER_AT[0] + 0.1
    arrive(us[2], ax.v, 1)
    along_v(ax.chunk(out, us[2], ax.v, cols), us[2], 2)
    yield base + GATHER_AT[2]
    for r in range(4):
        if r == 1:
            yield base + GATHER_AT[1]
            arrive(us[3], ax.v, 2)
            along_v(ax.chunk(out, us[3], ax.v, cols), us[3], 3)
            yield base + GATHER_AT[2] + GATHER_AT[3]
        v = wrap(ax.v - s)
        arrive(us[r], v, 3 + 3 * r)
        send(ax.chunk(out, us[r], v, cols), us[r], v, ax.device(v=wrap(ax.v + s)), 5 + 3 * r)
        yield base + GATHER_AT[2] + GATHER_AT[3] * r + 0.1
        arrive(us[r], wrap(ax.v + s), 4 + 3 * r)
        yield base + GATHER_AT[2] + GATHER_AT[3] * (r + 1)
    for r in range(4):
        yield base + GATHER_AT[2] + GATHER_AT[3] * r + GATHER_AT[4]
        arrive(us[r], wrap(ax.v + 2), 5 + 3 * r)
    yield 90
    for copy in sent:
        copy.wait_send()
    theirs = [ax.u, wrap(ax.u + s), wrap(ax.u - s), wrap(ax.u + 2)]
    landing = [(theirs[1], ax.v), (theirs[2], ax.v), (theirs[3], ax.v)]
    for r in range(4):
        landing += [(theirs[r], wrap(ax.v + s)), (theirs[r], wrap(ax.v - s)), (theirs[r], wrap(ax.v + 2))]
    for k, (u, v) in enumerate(landing):
        here = ax.chunk(out, u, v, ax.theirs)
        remote(here, here, chip_send.at[k], chip_recv.at[k], place.partner()).wait_recv()


def gather_stream(place, own, out, scratch, base=0):
    other, both, sems, local = scratch
    n = own.shape[1]
    yield from merge_own(place, own, other, both, sems.at[0, 0, 0, 15], sems.at[0, 0, 1, 15])
    keep = pltpu.make_async_copy(both, out.at[place.y, place.x], local)
    keep.start()
    yield from merge(
        [
            gather_half(
                Axes(place, h, n), both, out, base,
                sems.at[h, 0, 0], sems.at[h, 0, 1], sems.at[h, 1, 0], sems.at[h, 1, 1],
            )
            for h in (0, 1)
        ]
    )
    keep.wait()


def gather_scratch(n):
    return [
        pltpu.VMEM((36, n), BF16),
        pltpu.VMEM((CHUNK, n), BF16),
        pltpu.SemaphoreType.DMA((2, 2, 2, 16)),
        pltpu.SemaphoreType.DMA,
    ]


def add_chunks(count, target, *terms):
    def body(i, carry):
        total = terms[0](i)[...].astype(F32)
        for term in terms[1:]:
            total = total + term(i)[...].astype(F32)
        target(i)[...] = total.astype(BF16)
        return carry

    if count == 1:
        body(0, 0)
    else:
        lax.fori_loop(0, count, body, 0)


def scatter_half(ax, grads, final, bufs, sems, base):
    held, got, b1, b2, b3, c1, c2, c3, total = bufs
    place, s = ax.place, ax.place.s
    vs = [wrap(ax.v + 2), wrap(ax.v - s), wrap(ax.v + s), ax.v]
    for_partner = [wrap(ax.v + 2), wrap(ax.v + s), wrap(ax.v - s), ax.v]
    sent, loads, gets = [], [], []
    for k in range(4):
        yield 0.1 * k
        give = remote(
            ax.group(grads, for_partner[k], ax.theirs),
            got.at[k],
            sems.at[0, k],
            sems.at[1, k],
            place.partner(),
        )
        give.start()
        sent.append(give)
        gets.append(give)
        load = pltpu.make_async_copy(ax.group(grads, vs[k], ax.mine), held.at[k], sems.at[2, k])
        load.start()
        loads.append(load)
    yield base + SCATTER_AT[0]

    def chip_sum(k):
        loads[k].wait()
        gets[k].wait_recv()
        add_chunks(4, lambda i: got.at[k, i], lambda i: got.at[k, i], lambda i: held.at[k, i])

    def send(src, dst, k, device):
        copy = remote(src, dst, sems.at[0, k], sems.at[1, k], device)
        copy.start()
        sent.append(copy)
        return copy

    chip_sum(0)
    far = [
        send(got.at[0, pl.ds(2 * i, 2)], b1.at[pl.ds(2 * i, 2)], 4 + i, ax.device(v=wrap(ax.v + s)))
        for i in (0, 1)
    ]
    yield base + SCATTER_AT[1]
    chip_sum(1)
    back = send(got.at[1], b2, 6, ax.device(v=wrap(ax.v - s)))
    yield base + SCATTER_AT[2]
    chip_sum(2)
    forth = []
    for i in (0, 1):
        yield base + SCATTER_AT[3 + i]
        far[i].wait_recv()
        add_chunks(2, lambda k: b1.at[2 * i + k], lambda k: b1.at[2 * i + k], lambda k: got.at[2, 2 * i + k])
        forth.append(
            send(b1.at[pl.ds(2 * i, 2)], b3.at[pl.ds(2 * i, 2)], 7 + i, ax.device(v=wrap(ax.v + s)))
        )
    yield base + SCATTER_AT[5]
    loads[3].wait()
    gets[3].wait_recv()
    back.wait_recv()
    yield base + SCATTER_AT[6]
    for move in forth:
        move.wait_recv()
    add_chunks(
        4,
        lambda i: total.at[i],
        lambda i: got.at[3, i],
        lambda i: held.at[3, i],
        lambda i: b2.at[i],
        lambda i: b3.at[i],
    )
    far = send(total.at[wrap(ax.u + 2)], c1, 9, ax.device(u=wrap(ax.u + s)))
    back = send(total.at[wrap(ax.u - s)], c2, 10, ax.device(u=wrap(ax.u - s)))
    yield base + SCATTER_AT[7]
    far.wait_recv()
    add_chunks(1, lambda i: c1, lambda i: c1, lambda i: total.at[wrap(ax.u + s)])
    forth = send(c1, c3, 11, ax.device(u=wrap(ax.u + s)))
    back.wait_recv()
    yield base + SCATTER_AT[8]
    forth.wait_recv()
    add_chunks(1, lambda i: c2, lambda i: total.at[ax.u], lambda i: c2, lambda i: c3)
    keep = pltpu.make_async_copy(c2, final.at[:, ax.mine], sems.at[2, 4])
    keep.start()
    last = send(c2, final.at[:, ax.mine], 12, place.partner())
    yield 90
    for copy in sent:
        copy.wait_send()
    keep.wait()
    remote(c2, final.at[:, ax.theirs], sems.at[0, 12], sems.at[1, 12], place.partner()).wait_recv()


def scatter_scratch(n):
    shapes = []
    for w in halves(n):
        shapes += [pltpu.VMEM((4, 4, CHUNK, w), BF16)] * 2
        shapes += [pltpu.VMEM((4, CHUNK, w), BF16)] * 3
        shapes += [pltpu.VMEM((CHUNK, w), BF16)] * 3
        shapes += [pltpu.VMEM((4, CHUNK, w), BF16)]
        shapes += [pltpu.SemaphoreType.DMA((3, 13))]
    return shapes


def scatter_streams(place, grads, final, scratch, base=0):
    n = grads.shape[3]
    for h in (0, 1):
        part = scratch[10 * h : 10 * h + 10]
        yield scatter_half(Axes(place, h, n), grads, final, part[:9], part[9], base)


HALVES = (pl.ds(0, 80), pl.ds(80, 80))


def rows_gather(place, out, sems, base=0):
    s, z = place.s, place.z
    ahead, behind = place.device(z=wrap(z + s)), place.device(z=wrap(z - s))

    def copy(slot, rows, k, device):
        here = out.at[slot, rows]
        return remote(here, here, sems.at[0, k], sems.at[1, k], device)

    sent = [copy(z, HALVES[i], i, ahead) for i in (0, 1)] + [copy(z, HALVES[i], 2 + i, behind) for i in (0, 1)]
    for move in sent:
        move.start()
    for i in (0, 1):
        yield base + ROWS_AT[i]
        copy(wrap(z - s), HALVES[i], i, ahead).wait_recv()
        relay = copy(wrap(z - s), HALVES[i], 4 + i, ahead)
        relay.start()
        sent.append(relay)
    for i in (0, 1):
        yield base + ROWS_AT[2]
        copy(wrap(z + s), HALVES[i], 2 + i, ahead).wait_recv()
    for i in (0, 1):
        yield base + ROWS_AT[3 + i]
        copy(wrap(z + 2), HALVES[i], 4 + i, ahead).wait_recv()
    for move in sent:
        move.wait_send()


def rows_scatter(place, parts, bufs, sems):
    s, z = place.s, place.z
    b1, b2, b3 = bufs
    ahead, behind = place.device(z=wrap(z + s)), place.device(z=wrap(z - s))

    def copy(src, dst, rows, k, device):
        return remote(src.at[rows], dst.at[rows], sems.at[0, k], sems.at[1, k], device)

    far = [copy(parts.at[wrap(z + 2)], b1, HALVES[i], i, ahead) for i in (0, 1)]
    back = [copy(parts.at[wrap(z - s)], b2, HALVES[i], 2 + i, behind) for i in (0, 1)]
    forth = [copy(b1, b3, HALVES[i], 4 + i, ahead) for i in (0, 1)]
    for move in far + back:
        move.start()
    mid = wrap(z + s)

    def body(i, carry):
        rows = pl.ds(pl.multiple_of(i * 16, 16), 16)
        b1[rows, :] = (b1[rows, :].astype(F32) + parts[mid, rows, :].astype(F32)).astype(BF16)
        return carry

    for i in (0, 1):
        yield ROWS_AT[i]
        far[i].wait_recv()
        lax.fori_loop(5 * i, 5 * i + 5, body, 0)
        forth[i].start()
    yield ROWS_AT[2]
    for move in back:
        move.wait_recv()
    for i in (0, 1):
        yield ROWS_AT[3 + i]
        forth[i].wait_recv()
    for move in far + back + forth:
        move.wait_send()


def rows_scratch():
    return [pltpu.VMEM((ROWS, WIDTH), BF16)] * 3 + [pltpu.SemaphoreType.DMA((2, 6))] * 2


def row_blocks(body):
    def step(i, carry):
        body(pl.ds(pl.multiple_of(i * 16, 16), 16))
        return carry

    lax.fori_loop(0, ROWS // 16, step, 0)


def col_sum(ref, row, values):
    ref[8 * row : 8 * row + 8, :] = ref[8 * row : 8 * row + 8, :] + values[:8] + values[8:]


def start_kernel(tokens, attn_own, own_g, rows_out, mats_out, full_g, sems, *scratch):
    place = Place()
    place.greet(True)

    def z_stream():
        rows_out[place.z] = tokens[...]
        yield from rows_gather(place, rows_out, sems)

    run_streams(
        [
            gather_stream(place, attn_own, mats_out, scratch[:4]),
            gather_stream(place, own_g, full_g, scratch[4:8], 0.5),
            z_stream(),
        ]
    )


def middle_kernel(parts, tokens, gains, own_u, own_d, rows_out, attn_sum, full_u, full_d, *scratch):
    place = Place()
    place.greet(True)
    b1, b2, b3, sems, sems2 = scratch[:5]

    def z_stream():
        yield from rows_scatter(place, parts, (b1, b2, b3), sems)

        def body(rows):
            total = (
                parts[place.z, rows, :].astype(F32) + b2[rows, :].astype(F32) + b3[rows, :].astype(F32)
            )
            attn_sum[rows, :] = total
            hat, _ = normalize(total)
            hidden = tokens[rows, :].astype(F32) + hat * gains[1:2, :]
            mid, _ = normalize(hidden)
            rows_out[place.z, rows, :] = (mid * gains[2:3, :]).astype(BF16)

        row_blocks(body)
        yield from rows_gather(place, rows_out, sems2, 18)

    run_streams(
        [
            z_stream(),
            gather_stream(place, own_u, full_u, scratch[5:9]),
            gather_stream(place, own_d, full_d, scratch[9:13], 0.5),
        ]
    )


def turn_kernel(
    parts, tokens, attn_sum, gains, cotangent, gate, upward, rows_out, layer_out, sums, by_gate, by_up, *scratch
):
    place = Place()
    place.greet(False)
    b1, b2, b3, sems, sems2 = scratch[:5]
    sums[...] = jnp.zeros_like(sums)

    def z_stream():
        yield from rows_scatter(place, parts, (b1, b2, b3), sems)

        def body(rows):
            total = (
                parts[place.z, rows, :].astype(F32) + b2[rows, :].astype(F32) + b3[rows, :].astype(F32)
            )
            attn_hat, _ = normalize(attn_sum[rows, :])
            hidden = tokens[rows, :].astype(F32) + attn_hat * gains[1:2, :]
            hat, inverse = normalize(total)
            layer_out[rows, :] = (hidden + hat * gains[3:4, :]).astype(BF16)
            grad = cotangent[rows, :].astype(F32)
            col_sum(sums, 0, grad * hat)
            rows_out[place.z, rows, :] = normalize_back(grad * gains[3:4, :], hat, inverse).astype(BF16)

        row_blocks(body)
        yield from rows_gather(place, rows_out, sems2, 18)

    held_g, held_u, moves = scratch[5:8]

    def gelu_stream():
        def load(i):
            return (
                pltpu.make_async_copy(gate.at[i], held_g.at[i], moves.at[0, i]),
                pltpu.make_async_copy(upward.at[i], held_u.at[i], moves.at[1, i]),
            )

        def store(i):
            return (
                pltpu.make_async_copy(held_g.at[i], by_gate.at[i], moves.at[0, i]),
                pltpu.make_async_copy(held_u.at[i], by_up.at[i], moves.at[1, i]),
            )

        for i in range(8):
            for copy in load(i):
                copy.start()
        for i in range(8):
            yield (1 + i if i < 4 else 7 + i)
            for copy in load(i):
                copy.wait()

            def step(k, carry):
                rows = pl.ds(pl.multiple_of(k * 8, 8), 8)
                value, slope = gelu_parts(held_g[i, rows, :])
                held_g[i, rows, :] = held_u[i, rows, :] * slope
                held_u[i, rows, :] = value
                return carry

            lax.fori_loop(0, 10, step, 0)
            for copy in store(i):
                copy.start()
        yield 80
        for i in range(8):
            for copy in store(i):
                copy.wait()

    run_streams([z_stream(), gelu_stream()])


def back_kernel(
    parts, tokens, attn_sum, gains, cotangent, grad_d, grad_g,
    rows_out, grad_hidden, sums, sum_d, sum_g, *scratch
):
    place = Place()
    place.greet(True)
    b1, b2, b3, sems, sems2 = scratch[:5]
    sums[...] = jnp.zeros_like(sums)

    def z_stream():
        yield from rows_scatter(place, parts, (b1, b2, b3), sems)

        def body(rows):
            grad_mid = (
                parts[place.z, rows, :].astype(F32) + b2[rows, :].astype(F32) + b3[rows, :].astype(F32)
            )
            attn_hat, attn_inverse = normalize(attn_sum[rows, :])
            hidden = tokens[rows, :].astype(F32) + attn_hat * gains[1:2, :]
            mid, inverse = normalize(hidden)
            col_sum(sums, 0, grad_mid * mid)
            grad = cotangent[rows, :].astype(F32) + normalize_back(grad_mid * gains[2:3, :], mid, inverse)
            grad_hidden[rows, :] = grad
            col_sum(sums, 1, grad * attn_hat)
            rows_out[place.z, rows, :] = normalize_back(
                grad * gains[1:2, :], attn_hat, attn_inverse
            ).astype(BF16)

        row_blocks(body)
        yield from rows_gather(place, rows_out, sems2, 18)

    streams = [z_stream()]
    for i, (grads, final) in enumerate(((grad_d, sum_d), (grad_g, sum_g))):
        streams += list(scatter_streams(place, grads, final, scratch[5 + 20 * i : 25 + 20 * i], 0.5 * i))
    run_streams(streams)


def end_kernel(parts, grads, grad_u, grad_rows, final, shared, sum_u, *scratch):
    place = Place()
    place.greet(True, far_z=True)
    b1, b2, b3, sems, sems2 = scratch[:5]
    got, zsend, zrecv = scratch[5:8]

    def z_stream():
        yield from rows_scatter(place, parts, (b1, b2, b3), sems)

        def body(rows):
            grad_rows[rows, :] = (
                parts[place.z, rows, :].astype(F32) + b2[rows, :].astype(F32) + b3[rows, :].astype(F32)
            )

        row_blocks(body)

    def attn_stream():
        yield from merge(scatter_streams(place, grads, final, scratch[8:28]))
        cols = pl.ds(512, 768)
        copies = []
        for k in range(3):
            copy = remote(
                final.at[:, cols], got.at[k], zsend.at[k], zrecv.at[k], place.device(z=wrap(place.z + k + 1))
            )
            copy.start()
            copies.append(copy)
        yield 95
        for copy in copies:
            copy.wait()
        total = final[:, cols].astype(F32)
        for k in range(3):
            total = total + got[k].astype(F32)
        shared[...] = total

    run_streams([attn_stream(), z_stream()] + list(scatter_streams(place, grad_u, sum_u, scratch[28:48], 0.5)))


def call(kernel, outs, ins, spaces, out_spaces, scratch, ident, name=None):
    return pl.pallas_call(
        kernel,
        out_shape=[jax.ShapeDtypeStruct(shape, dtype) for shape, dtype in outs],
        in_specs=[pl.BlockSpec(memory_space=space) for space in spaces],
        out_specs=[pl.BlockSpec(memory_space=space) for space in out_spaces],
        scratch_shapes=scratch,
        compiler_params=pltpu.CompilerParams(
            collective_id=ident, has_side_effects=True, vmem_limit_bytes=60 * 1024 * 1024
        ),
        name=name or kernel.__name__,
    )(*ins)


def local(
    tokens,
    cotangent,
    segment_ids,
    positions,
    w_query,
    w_key,
    w_value,
    w_out,
    w_gate,
    w_up,
    w_down,
    prenorm_attn,
    postnorm_attn,
    prenorm_ffw,
    postnorm_ffw,
    query_norm,
    key_norm,
):
    vm, hbm = pltpu.VMEM, pl.ANY
    shard = 36
    core = lax.rem(lax.axis_index("dp"), 2)
    hidden_units = w_gate.shape[1]
    pad = ((0, 0), (0, FFPAD - hidden_units))
    width = w_key.shape[1]

    vectors = jnp.stack(
        [
            jnp.pad(g, (0, shard - g.shape[0]))
            for g in (prenorm_attn, postnorm_attn, prenorm_ffw, postnorm_ffw, query_norm, key_norm)
        ]
    )
    spread = jnp.eye(6, 256, dtype=BF16)
    attn_own = jnp.concatenate(
        [w_query, w_out.T, w_key, w_value, contract_rows(vectors, spread).astype(BF16)], axis=1
    )
    whole = ((4, 4, CHUNK, FFPAD), BF16)
    tokens_all, mats, full_gate = call(
        start_kernel,
        [((4, ROWS, WIDTH), BF16), ((4, 4, CHUNK, ATTN_COLS), BF16), whole],
        [tokens, attn_own, jnp.pad(w_gate, pad)],
        [vm, vm, vm],
        [vm, hbm, hbm],
        [pltpu.SemaphoreType.DMA((2, 6))] + gather_scratch(ATTN_COLS) + gather_scratch(FFPAD),
        0,
    )
    mats = mats.reshape(WIDTH, ATTN_COLS)
    full_query, full_out = mats[:, :256], mats[:, 256:512]
    full_key, full_value = mats[:, 512:768], mats[:, 768:1024]
    small = mats[:, 1024:1032].astype(F32).T
    gains = small
    gain_in = small[0]
    gain_query = small[4].reshape(32, shard)[:, :8].reshape(-1)
    gain_key = small[5].reshape(32, shard)[:, :8].reshape(-1)
    normed_all, _ = normalize(tokens_all.reshape(4 * ROWS, WIDTH).astype(F32))
    attn_rows = (normed_all * gain_in).astype(BF16)
    scale = 1.0 / math.sqrt(width)
    cosine, sine = rotary_tables(positions.reshape(-1), width)
    mask = window_mask(segment_ids[0])
    key_hat, key_inverse = normalize(jnp.dot(attn_rows, full_key, preferred_element_type=F32))
    keys = rotate(key_hat * gain_key, cosine, sine).astype(BF16)
    values = jnp.dot(attn_rows, full_value, preferred_element_type=F32).astype(BF16)
    query_hat, query_inverse = normalize(jnp.dot(attn_rows, full_query, preferred_element_type=F32))
    queries = rotate(query_hat * gain_query, cosine, sine).astype(BF16)
    piece, logsum = attend_forward(queries, keys, values, mask, scale)
    heads_out = piece.astype(BF16)
    attn_part = contract_cols(heads_out, full_out).astype(BF16)
    ffw_rows, attn_sum, full_up, full_down = call(
        middle_kernel,
        [((4, ROWS, WIDTH), BF16), ((ROWS, WIDTH), F32), whole, whole],
        [
            attn_part.reshape(4, ROWS, WIDTH),
            tokens,
            gains,
            jnp.pad(w_up, pad),
            jnp.pad(w_down.T, pad),
        ],
        [vm] * 5,
        [vm, vm, hbm, hbm],
        rows_scratch() + gather_scratch(FFPAD) * 2,
        1,
    )
    ffw_rows = ffw_rows.reshape(4 * ROWS, WIDTH)
    full_gate = full_gate.reshape(WIDTH, FFPAD)
    full_up = full_up.reshape(WIDTH, FFPAD)
    full_down = full_down.reshape(WIDTH, FFPAD)
    gate = jnp.dot(ffw_rows, full_gate, preferred_element_type=F32)
    upward = jnp.dot(ffw_rows, full_up, preferred_element_type=F32)
    gelu_value, _ = gelu_parts(gate)
    act = (gelu_value * upward).astype(BF16)
    ffw_part = contract_cols(act, full_down).astype(BF16)
    blocks = (8, 80, FFPAD)
    grad_ffw, layer_out, ffw_sums, by_gate, by_up = call(
        turn_kernel,
        [((4, ROWS, WIDTH), BF16), ((ROWS, WIDTH), BF16), ((8, WIDTH), F32), (blocks, F32), (blocks, F32)],
        [
            ffw_part.reshape(4, ROWS, WIDTH),
            tokens,
            attn_sum,
            gains,
            cotangent,
            gate.reshape(blocks),
            upward.reshape(blocks),
        ],
        [vm] * 5 + [hbm] * 2,
        [vm] * 3 + [hbm] * 2,
        rows_scratch() + [pltpu.VMEM(blocks, F32)] * 2 + [pltpu.SemaphoreType.DMA((2, 8))],
        2,
    )
    grad_ffw = grad_ffw.reshape(4 * ROWS, WIDTH)
    grad_down = contract_rows(grad_ffw, act).astype(BF16)
    grad_act = jnp.dot(grad_ffw, full_down, preferred_element_type=F32)
    grad_gate_in = (grad_act * by_gate.reshape(4 * ROWS, FFPAD)).astype(BF16)
    grad_up_in = (grad_act * by_up.reshape(4 * ROWS, FFPAD)).astype(BF16)
    grad_gate = contract_rows(ffw_rows, grad_gate_in).astype(BF16)
    grad_up = contract_rows(ffw_rows, grad_up_in).astype(BF16)
    mid_part = (contract_cols(grad_gate_in, full_gate) + contract_cols(grad_up_in, full_up)).astype(BF16)
    split = (4, 4, CHUNK, FFPAD)
    final = ((CHUNK, FFPAD), BF16)
    grad_attn, grad_hidden, mid_sums, sum_down, sum_gate = call(
        back_kernel,
        [((4, ROWS, WIDTH), BF16), ((ROWS, WIDTH), F32), ((16, WIDTH), F32), final, final],
        [
            mid_part.reshape(4, ROWS, WIDTH),
            tokens,
            attn_sum,
            gains,
            cotangent,
            grad_down.reshape(split),
            grad_gate.reshape(split),
        ],
        [vm] * 5 + [hbm] * 2,
        [vm] * 5,
        rows_scratch() + scatter_scratch(FFPAD) * 2,
        3,
    )
    grad_attn = grad_attn.reshape(4 * ROWS, WIDTH)
    grad_output = contract_rows(grad_attn, heads_out)
    grad_heads = jnp.dot(grad_attn, full_out, preferred_element_type=F32).astype(BF16)
    grad_queries, grad_keys, grad_values = attend_backward(
        queries, keys, values, mask, scale, logsum, grad_heads
    )
    grad_query_turned = rotate(grad_queries, cosine, -sine)
    grad_query_norm = jnp.sum(grad_query_turned * query_hat, axis=0)
    query_in = normalize_back(grad_query_turned * gain_query, query_hat, query_inverse).astype(BF16)
    grad_key_turned = rotate(grad_keys, cosine, -sine)
    grad_key_norm = jnp.sum(grad_key_turned * key_hat, axis=0)
    key_in = normalize_back(grad_key_turned * gain_key, key_hat, key_inverse).astype(BF16)
    value_in = grad_values.astype(BF16)
    in_part = contract_cols(query_in, full_query)
    in_part = in_part + contract_cols(key_in, full_key)
    in_part = in_part + contract_cols(value_in, full_value)
    grad_pre_attn = jnp.sum(in_part * normed_all, axis=0)

    def placed_rows(vector):
        return jnp.pad(vector.reshape(32, 8), ((0, 0), (0, shard - 8))).reshape(-1)

    vectors = jnp.stack(
        [
            grad_pre_attn,
            jnp.sum(mid_sums[8:], axis=0),
            jnp.sum(mid_sums[:8], axis=0),
            jnp.sum(ffw_sums, axis=0),
            placed_rows(grad_query_norm),
            placed_rows(grad_key_norm),
        ]
    )
    small_grads = contract_rows(vectors.astype(BF16), spread)
    grad_qkv = contract_rows(attn_rows, jnp.concatenate([query_in, key_in, value_in], axis=1))
    grads = jnp.concatenate(
        [g.astype(BF16) for g in (grad_qkv[:, :256], grad_output, grad_qkv[:, 256:], small_grads)], axis=1
    )
    grad_in_rows, sum_attn, sum_shared, sum_up = call(
        end_kernel,
        [((ROWS, WIDTH), F32), ((CHUNK, ATTN_COLS), BF16), ((CHUNK, ATTN_COLS - 512), F32), final],
        [
            in_part.astype(BF16).reshape(4, ROWS, WIDTH),
            grads.reshape(4, 4, CHUNK, ATTN_COLS),
            grad_up.reshape(split),
        ],
        [vm, hbm, hbm],
        [vm] * 4,
        rows_scratch()
        + [
            pltpu.VMEM((3, CHUNK, ATTN_COLS - 512), BF16),
            pltpu.SemaphoreType.DMA((3,)),
            pltpu.SemaphoreType.DMA((3,)),
        ]
        + scatter_scratch(ATTN_COLS)
        + scatter_scratch(FFPAD),
        4,
    )
    normed_in, inverse_in = normalize(tokens.astype(F32))
    grad_tokens = grad_hidden + normalize_back(grad_in_rows * gain_in, normed_in, inverse_in)

    def own_rows(array):
        first = core == 0
        return jnp.where(first, array[:shard], array[shard:]).astype(F32)

    own_attn = own_rows(sum_attn[:, :512])
    own_shared = own_rows(sum_shared)
    own_small = own_shared[:, 512:520]
    return (
        layer_out,
        grad_tokens,
        own_attn[:, :256],
        own_shared[:, :256],
        own_shared[:, 256:512],
        own_attn[:, 256:].T,
        own_rows(sum_gate)[:, :hidden_units],
        own_rows(sum_up)[:, :hidden_units],
        own_rows(sum_down)[:, :hidden_units].T,
        own_small[:, 0],
        own_small[:, 1],
        own_small[:, 2],
        own_small[:, 3],
        own_small[:8, 4],
        own_small[:8, 5],
    )


def solution(mesh):
    placed = (
        P(("dp", "tensor"), None),
        P(("dp", "tensor"), None),
        P("dp", None),
        P("dp", None),
        P("dp", "tensor"),
        P("dp", None),
        P("dp", None),
        P("tensor", "dp"),
        P("dp", "tensor"),
        P("dp", "tensor"),
        P("tensor", "dp"),
        P("dp"),
        P("dp"),
        P("dp"),
        P("dp"),
        P("dp"),
        P("dp"),
    )
    return jax.shard_map(
        local,
        mesh=mesh,
        in_specs=placed,
        out_specs=(
            P(("dp", "tensor"), None),
            P(("dp", "tensor"), None),
            P("dp", "tensor"),
            P("dp", None),
            P("dp", None),
            P("tensor", "dp"),
            P("dp", "tensor"),
            P("dp", "tensor"),
            P("tensor", "dp"),
            P("dp"),
            P("dp"),
            P("dp"),
            P("dp"),
            P("dp"),
            P("dp"),
        ),
        check_vma=False,
    )
```
